32 devices in a mesh: dp: 2 (over y), row: 4 (over z), col: 4 (over x, core).
Axes of the slice: x: 2, y: 2, z: 4, core: 2. Of those that a mesh axis runs over, the one named last changes fastest.
Arguments:
- block_input: bfloat16 [1024, 1024], P(('dp', 'col'), 'row'), may hold values from -6 to 6
- attn_gain: float32 [1024], P('row'), may hold values from 0.25 to 1.75
- w_qkv: bfloat16 [1024, 2048], P('row', 'col'), may hold values from -0.1875 to 0.1875
- w_out: bfloat16 [1024, 1024], P('col', 'row'), may hold values from -0.75 to 0.75
- ffn_gain: float32 [1024], P('row'), may hold values from 0.25 to 1.75
- w_router: float32 [1024, 32], P('row'), may hold values from -0.0625 to 0.0625
- w_gate: bfloat16 [32, 1024, 512], P(None, 'row', 'col'), may hold values from -0.1875 to 0.1875
- w_up: bfloat16 [32, 1024, 512], P(None, 'row', 'col'), may hold values from -0.1875 to 0.1875
- w_down: bfloat16 [32, 512, 1024], P(None, 'col', 'row'), may hold values from -0.25 to 0.25
- routes: int32 [1024, 8], P('dp'), may hold values from 0 to 31, all different within a row; in each aligned block of 512 rows (0 to 511, 512 to 1023, ...) at most 192 rows name the same one
- out_grad: bfloat16 [1024, 1024], P(('dp', 'col'), 'row'), may hold values from -6 to 6
Outputs:
- block_output: bfloat16 [1024, 1024], P(('dp', 'col'), 'row')
- input_grad: float32 [1024, 1024], P(('dp', 'col'), 'row')
- grad_attn_gain: float32 [1024], P('row')
- grad_qkv: float32 [1024, 2048], P('row', 'col')
- grad_out: float32 [1024, 1024], P('col', 'row')
- grad_ffn_gain: float32 [1024], P('row')
- grad_router: float32 [1024, 32], P('row')
- grad_gate: float32 [32, 1024, 512], P('dp', 'row', 'col')
- grad_up: float32 [32, 1024, 512], P('dp', 'row', 'col')
- grad_down: float32 [32, 512, 1024], P('dp', 'col', 'row')
The draws below stay inside these ranges and needn't reach their ends.
Inputs may be any that keep to these rules, and one draw needn't show every extreme that they name: `routes`: every row names 8 different experts. Among the 512 rows of one sequence no expert is named more than 192 times, a bound that some block reaches.
All inputs are finite; a program needn't handle non-finite values.
Results may differ from the reference program's by a relative error of at most 0.013.
Values may be sent and summed in bfloat16 or wider, within the bound.
A program may use at most 128 MiB of HBM per device.

```python
import math
import jax
import jax.numpy as jnp
import numpy as np
from jax import lax

D = 1024
HEADS = 16
KV_HEADS = 8
HEAD_DIM = 64
EXPERTS = 32
FF = 512
TOPK = 8
SEQ = 512
CAP = 192
TOKENS = 1024


def steps_of(stream_key, dims, split, low, largest):
    level, own = 1.0, jax.random.fold_in(stream_key, 6)
    for dim, blocks in split:
        steps = jnp.exp(jax.random.uniform(jax.random.fold_in(own, dim), (blocks,), jnp.float32, low / len(split), largest / len(split)))
        level = level * jnp.repeat(steps, dims[dim] // blocks).reshape([-1 if axis == dim else 1 for axis in range(len(dims))])
    return level


def routed_block(rng, own, number, rows, number_of, top, reach, lean):
    sequence = jax.random.permutation(rng, number_of)
    crowded, usual = portions_of(number_of, rows * top, reach, lean, True), portions_of(number_of, rows * top, reach, lean, False)
    places = jnp.arange(number_of)

    def named(sizes, turn):
        used = int((sizes > 0).sum())
        fixed = max(1, used // 4)
        moved = fixed + (places - fixed + turn * (used - fixed)) % max(1, number_of - fixed)
        return jnp.zeros((number_of,), jnp.int32).at[sequence[jnp.where(places < fixed, places, moved)]].set(jnp.asarray(sizes, jnp.int32))

    sizes = jnp.where(number % 4 == 0, named(crowded, number // 4), named(usual, number - number // 4 - 1))
    mixed = jax.random.permutation(jax.random.fold_in(own, 3), number_of)
    donor, receiver = mixed[0:number_of // 2 * 2:2], mixed[1:number_of // 2 * 2:2]
    room = jnp.minimum(sizes[donor] - 1, reach - sizes[receiver]) // 2
    room = jnp.where((donor == sequence[0]) | (receiver == sequence[0]) | (sizes[receiver] == 0), 0, jnp.maximum(room, 0))
    moved = jax.random.randint(jax.random.fold_in(own, 4), (number_of // 2,), 0, 1 << 20) % (room + 1)
    sizes = sizes.at[donor].add(-moved).at[receiver].add(moved)
    members = jnp.searchsorted(jnp.cumsum(sizes), jnp.arange(rows * top), side="right").astype(jnp.int32)
    listing = members.reshape(top, rows).T
    listing = listing[jax.random.permutation(jax.random.fold_in(own, 1), rows)]
    turn = jax.random.randint(jax.random.fold_in(own, 2), (rows, 1), 0, top)
    return jnp.take_along_axis(listing, (jnp.arange(top)[None, :] + turn) % top, axis=1)


def portions_of(number_of, total, bound, lean, full):
    loads = [(1 << 20) // math.isqrt(rank ** lean) + 1 for rank in range(1, number_of + 1)]
    largest = bound if full else min(bound, max(-(-total // number_of), total * loads[0] // sum(loads)))
    least = 1 if total - largest >= number_of - 1 else 0
    holding, rest = [largest] + [least] * (number_of - 1), total - largest - least * (number_of - 1)
    while rest > 0:
        free = [i for i in range(1, number_of) if holding[i] < largest] or [i for i in range(1, number_of) if holding[i] < bound]
        mass, left = sum([loads[i] for i in free]), rest
        for i in free:
            more = min(bound - holding[i], max(1, left * loads[i] // mass), rest)
            holding[i] = holding[i] + more
            rest = rest - more
    return np.array(holding)


def gaussian(own_key, dims, spread, reach, cuts=(), held_as=jnp.bfloat16):
    values = spread * jax.random.normal(own_key, dims, jnp.float32)
    if cuts:
        values = values * steps_of(own_key, dims, cuts, -0.22, 0.18)
    return jnp.clip(values, -reach, reach).astype(held_as)


def setup_inputs(seed: int = 0) -> dict:
    seeds = jax.random.split(jax.random.key(seed), 12)
    block_input = gaussian(seeds[0], (TOKENS, D), 1.0, 6.0, ((0, 8), (1, 4)))
    attn_gain = jnp.clip(1.0 + 0.15 * jax.random.normal(seeds[1], (D,), jnp.float32), 0.25, 1.75)
    w_qkv = gaussian(seeds[2], (D, (HEADS + 2 * KV_HEADS) * HEAD_DIM), D ** -0.5, 0.1875, ((0, 4), (1, 4)))
    w_out = gaussian(seeds[3], (HEADS * HEAD_DIM, D), (D // 16) ** -0.5, 0.75, ((0, 4), (1, 4)))
    ffn_gain = jnp.clip(1.0 + 0.15 * jax.random.normal(seeds[4], (D,), jnp.float32), 0.25, 1.75)
    w_router = gaussian(seeds[5], (D, EXPERTS), (8 * D) ** -0.5, 0.0625, ((0, 4),), jnp.float32)
    w_gate = gaussian(seeds[6], (EXPERTS, D, FF), D ** -0.5, 0.1875, ((1, 4), (2, 4)))
    w_up = gaussian(seeds[7], (EXPERTS, D, FF), D ** -0.5, 0.1875, ((1, 4), (2, 4)))
    w_down = gaussian(seeds[8], (EXPERTS, FF, D), FF ** -0.5, 0.25, ((1, 4), (2, 4)))
    routes_keys = jax.random.split(jax.random.fold_in(seeds[9], 1), TOKENS // SEQ)
    routes_turns = jax.random.permutation(jax.random.fold_in(seeds[9], 3), TOKENS // SEQ)
    routes = jax.vmap(lambda own, number: routed_block(jax.random.fold_in(seeds[9], 2), own, number, SEQ, EXPERTS, TOPK, CAP, 2))(routes_keys, routes_turns).reshape((TOKENS, TOPK))
    out_grad = gaussian(seeds[10], (TOKENS, D), 1.0, 6.0, ((0, 8), (1, 4)))
    return {"block_input": block_input, "attn_gain": attn_gain, "w_qkv": w_qkv, "w_out": w_out, "ffn_gain": ffn_gain, "w_router": w_router, "w_gate": w_gate, "w_up": w_up, "w_down": w_down, "routes": routes, "out_grad": out_grad}


epsilon = 1e-06
rope_base = 10000.0

def rotate_half(head_values):
    half_width = head_values.shape[-1] // 2
    return jnp.concatenate([-head_values[..., half_width:], head_values[..., :half_width]], axis=-1)

def rope_tables(positions, head_dim):
    half_width = head_dim // 2
    inverse = rope_base ** (-jnp.arange(half_width, dtype=jnp.float32) / half_width)
    angles = positions.astype(jnp.float32)[:, None] * inverse[None, :]
    cos_table = jnp.cos(angles)
    sin_table = jnp.sin(angles)
    return (jnp.concatenate([cos_table, cos_table], axis=-1), jnp.concatenate([sin_table, sin_table], axis=-1))

def slot_tables(routes_seq, experts, capacity):
    flat_routes = routes_seq.reshape(-1)
    pair_count = flat_routes.shape[0]
    onehot = (flat_routes[:, None] == jnp.arange(experts, dtype=jnp.int32)[None, :]).astype(jnp.int32)
    before = jnp.cumsum(onehot, axis=0) - onehot
    rank_in_expert = lax.optimization_barrier(jnp.sum(before * onehot, axis=1))
    slot_of_pair = flat_routes * capacity + rank_in_expert
    pair_of_slot = jnp.zeros((experts * capacity,), jnp.int32).at[slot_of_pair].set(jnp.arange(pair_count, dtype=jnp.int32))
    filled = jnp.zeros((experts * capacity,), jnp.int32).at[slot_of_pair].set(1)
    return (slot_of_pair, pair_of_slot, filled)

def sequence_pass(seq_input, seq_routes, seq_grad, attn_gain, w_qkv, w_out, ffn_gain, w_router, w_both_f, w_down_f):
    repeat = HEADS // KV_HEADS
    score_scale = HEAD_DIM ** (-0.5)
    inputs_f = seq_input.astype(jnp.float32)
    inv_rms_one = lax.rsqrt(lax.optimization_barrier(jnp.mean(inputs_f * inputs_f, axis=1, keepdims=True)) + epsilon)
    unit_one = inputs_f * inv_rms_one
    normed_one = (unit_one * attn_gain).astype(jnp.bfloat16)
    proj_qkv = jnp.dot(normed_one, w_qkv, preferred_element_type=jnp.float32).reshape(SEQ, KV_HEADS, repeat + 2, HEAD_DIM)
    positions = jnp.arange(SEQ, dtype=jnp.int32)
    cos_table, sin_table = rope_tables(positions, HEAD_DIM)
    queries = proj_qkv[:, :, :repeat]
    keys_raw = proj_qkv[:, :, repeat]
    vals_raw = proj_qkv[:, :, repeat + 1]
    queries_rot = ((queries * cos_table[:, None, None] + rotate_half(queries) * sin_table[:, None, None]) * score_scale).astype(jnp.bfloat16)
    keys_rot = (keys_raw * cos_table[:, None] + rotate_half(keys_raw) * sin_table[:, None]).astype(jnp.bfloat16)
    values = vals_raw.astype(jnp.bfloat16)
    causal = positions[None, :] <= positions[:, None]
    scores = jnp.einsum('qgrd,kgd->grqk', queries_rot.astype(jnp.float32), keys_rot.astype(jnp.float32))
    exp_scores = jnp.where(causal, jnp.exp(scores), 0.0)
    log_total = jnp.log(lax.optimization_barrier(jnp.sum(exp_scores, axis=-1, keepdims=True)))
    attn_probs = jnp.where(causal, jnp.exp(scores - log_total), 0.0)
    probs_b = attn_probs.astype(jnp.bfloat16)
    attended = jnp.einsum('grqk,kgd->qgrd', probs_b.astype(jnp.float32), values.astype(jnp.float32)).astype(jnp.bfloat16).reshape(SEQ, HEADS * HEAD_DIM)
    hidden_res = inputs_f + jnp.dot(attended, w_out, preferred_element_type=jnp.float32)
    inv_rms_two = lax.rsqrt(lax.optimization_barrier(jnp.mean(hidden_res * hidden_res, axis=1, keepdims=True)) + epsilon)
    unit_two = hidden_res * inv_rms_two
    normed_two_f = unit_two * ffn_gain
    normed_two = normed_two_f.astype(jnp.bfloat16)
    logits = jnp.dot(normed_two_f, w_router, precision=lax.Precision.HIGHEST)
    chosen_mask = (seq_routes[:, :, None] == jnp.arange(EXPERTS, dtype=jnp.int32)[None, None, :]).astype(jnp.float32)
    chosen = lax.optimization_barrier(jnp.sum(chosen_mask * logits[:, None, :], axis=2))
    exp_chosen = jnp.exp(chosen)
    gate_weights = exp_chosen / lax.optimization_barrier(jnp.sum(exp_chosen, axis=1, keepdims=True))
    slot_of_pair, pair_of_slot, filled = slot_tables(seq_routes, EXPERTS, CAP)
    token_of_slot = pair_of_slot // TOPK
    slot_rows = jnp.where(filled[:, None] > 0, normed_two[token_of_slot], 0).astype(jnp.bfloat16)
    pre_act = jnp.einsum('ecd,edf->ecf', slot_rows.reshape(EXPERTS, CAP, D).astype(jnp.float32), w_both_f)
    gate_pre = pre_act[:, :, :FF]
    up_val = pre_act[:, :, FF:]
    sigmoid_gate = jax.nn.sigmoid(gate_pre)
    activated = (gate_pre * sigmoid_gate * up_val).astype(jnp.bfloat16)
    down_slots = jnp.einsum('ecf,efd->ecd', activated.astype(jnp.float32), w_down_f).reshape(EXPERTS * CAP, D)
    pair_out = down_slots[slot_of_pair].reshape(SEQ, TOPK, D)
    block_output = (hidden_res + lax.optimization_barrier(jnp.sum(gate_weights[:, :, None] * pair_out, axis=1))).astype(jnp.bfloat16)
    grad_f = seq_grad.astype(jnp.float32)
    gate_grads = lax.optimization_barrier(jnp.sum(grad_f[:, None, :] * pair_out, axis=2))
    gate_mix = gate_weights * (gate_grads - lax.optimization_barrier(jnp.sum(gate_weights * gate_grads, axis=1, keepdims=True)))
    logit_grads = lax.optimization_barrier(jnp.sum(gate_mix[:, :, None] * chosen_mask, axis=1))
    pair_grad = (gate_weights[:, :, None] * grad_f[:, None, :]).astype(jnp.bfloat16).reshape(SEQ * TOPK, D)
    slot_grad = jnp.where(filled[:, None] > 0, pair_grad[pair_of_slot], 0).astype(jnp.bfloat16).reshape(EXPERTS, CAP, D)
    act_grad = jnp.einsum('ecd,efd->ecf', slot_grad.astype(jnp.float32), w_down_f)
    gate_pre_grad = act_grad * up_val * sigmoid_gate * (1.0 + gate_pre * (1.0 - sigmoid_gate))
    up_grad = act_grad * gate_pre * sigmoid_gate
    pre_grad = jnp.concatenate([gate_pre_grad, up_grad], axis=2).astype(jnp.bfloat16)
    down_grad = jnp.einsum('ecf,ecd->efd', activated.astype(jnp.float32), slot_grad.astype(jnp.float32))
    both_grad = jnp.einsum('ecd,ecf->edf', slot_rows.reshape(EXPERTS, CAP, D).astype(jnp.float32), pre_grad.astype(jnp.float32))
    slot_back = jnp.einsum('ecf,edf->ecd', pre_grad.astype(jnp.float32), w_both_f).reshape(EXPERTS * CAP, D)
    normed_grad = lax.optimization_barrier(jnp.sum(slot_back[slot_of_pair].reshape(SEQ, TOPK, D), axis=1))
    normed_grad = normed_grad + jnp.dot(logit_grads, w_router.T, precision=lax.Precision.HIGHEST)
    ffn_gain_grad = lax.optimization_barrier(jnp.sum(normed_grad * unit_two, axis=0))
    router_grad = jnp.dot(normed_two_f.T, logit_grads, precision=lax.Precision.HIGHEST)
    unit_grad_two = normed_grad * ffn_gain
    residual_grad = grad_f + inv_rms_two * (unit_grad_two - unit_two * lax.optimization_barrier(jnp.mean(unit_grad_two * unit_two, axis=1, keepdims=True)))
    residual_b = residual_grad.astype(jnp.bfloat16)
    out_proj_grad = jnp.dot(attended.T, residual_b, preferred_element_type=jnp.float32)
    attended_grad = jnp.dot(residual_b, w_out.T, preferred_element_type=jnp.float32).astype(jnp.bfloat16).reshape(SEQ, KV_HEADS, repeat, HEAD_DIM)
    prob_grad = jnp.einsum('qgrd,kgd->grqk', attended_grad.astype(jnp.float32), values.astype(jnp.float32))
    prob_inner = lax.optimization_barrier(jnp.sum(attn_probs * prob_grad, axis=-1, keepdims=True))
    score_grad = (attn_probs * (prob_grad - prob_inner)).astype(jnp.bfloat16)
    query_grad = jnp.einsum('grqk,kgd->qgrd', score_grad.astype(jnp.float32), keys_rot.astype(jnp.float32))
    key_grad = jnp.einsum('grqk,qgrd->kgd', score_grad.astype(jnp.float32), queries_rot.astype(jnp.float32))
    value_grad = jnp.einsum('grqk,qgrd->kgd', probs_b.astype(jnp.float32), attended_grad.astype(jnp.float32))
    query_back = (query_grad * cos_table[:, None, None] - rotate_half(query_grad * sin_table[:, None, None])) * score_scale
    key_back = key_grad * cos_table[:, None] - rotate_half(key_grad * sin_table[:, None])
    qkv_grad = jnp.concatenate([query_back, key_back[:, :, None], value_grad[:, :, None]], axis=2).reshape(SEQ, -1).astype(jnp.bfloat16)
    qkv_weight_grad = jnp.dot(normed_one.T, qkv_grad, preferred_element_type=jnp.float32)
    normed_one_grad = jnp.dot(qkv_grad, w_qkv.T, preferred_element_type=jnp.float32)
    attn_gain_grad = lax.optimization_barrier(jnp.sum(normed_one_grad * unit_one, axis=0))
    unit_grad_one = normed_one_grad * attn_gain
    input_grad = residual_grad + inv_rms_one * (unit_grad_one - unit_one * lax.optimization_barrier(jnp.mean(unit_grad_one * unit_one, axis=1, keepdims=True)))
    grads = (attn_gain_grad, qkv_weight_grad, out_proj_grad, ffn_gain_grad, router_grad, both_grad[:, :, :FF], both_grad[:, :, FF:], down_grad)
    return ((block_output, input_grad), grads)

def reference(block_input, attn_gain, w_qkv, w_out, ffn_gain, w_router, w_gate, w_up, w_down, routes, out_grad):
    seq_count = block_input.shape[0] // SEQ
    w_both_f = jnp.concatenate([w_gate, w_up], axis=2).astype(jnp.float32)
    w_down_f = w_down.astype(jnp.float32)
    inputs = block_input.reshape(seq_count, SEQ, D)
    route_blocks = routes.reshape(seq_count, SEQ, TOPK)
    grad_blocks = out_grad.reshape(seq_count, SEQ, D)
    initial = (jnp.zeros((D,), jnp.float32), jnp.zeros(w_qkv.shape, jnp.float32), jnp.zeros(w_out.shape, jnp.float32), jnp.zeros((D,), jnp.float32), jnp.zeros((D, EXPERTS), jnp.float32), jnp.zeros((EXPERTS, D, FF), jnp.float32), jnp.zeros((EXPERTS, D, FF), jnp.float32), jnp.zeros((EXPERTS, FF, D), jnp.float32))

    def one_sequence(totals, pieces):
        seq_input, seq_routes, seq_grad = pieces
        outputs, grads = sequence_pass(seq_input, seq_routes, seq_grad, attn_gain, w_qkv, w_out, ffn_gain, w_router, w_both_f, w_down_f)
        return (jax.tree.map(jnp.add, totals, grads), outputs)
    totals, outputs = lax.scan(one_sequence, initial, (inputs, route_blocks, grad_blocks))
    block_output = outputs[0].reshape(seq_count * SEQ, D)
    input_grad = outputs[1].reshape(seq_count * SEQ, D)
    return (block_output, input_grad, totals[0], totals[1], totals[2], totals[3], totals[4], totals[5], totals[6], totals[7])
```

```python
import jax
import jax.numpy as jnp
from jax import lax
from jax.sharding import PartitionSpec as P

HEADS = 16
KV_HEADS = 8
HEAD_DIM = 64
CAP = 192
EXPERTS = 32


epsilon = 1e-06
rope_base = 10000.0


def rotate_half(head_values):
    half_width = head_values.shape[-1] // 2
    return jnp.concatenate([-head_values[..., half_width:], head_values[..., :half_width]], axis=-1)


def rope_tables(positions, head_dim):
    half_width = head_dim // 2
    inverse = rope_base ** (-jnp.arange(half_width, dtype=jnp.float32) / half_width)
    angles = positions.astype(jnp.float32)[:, None] * inverse[None, :]
    cos_table = jnp.cos(angles)
    sin_table = jnp.sin(angles)
    return (
        jnp.concatenate([cos_table, cos_table], axis=-1),
        jnp.concatenate([sin_table, sin_table], axis=-1),
    )


def slot_tables(routes_seq, experts, capacity):
    flat_routes = routes_seq.reshape(-1)
    pair_count = flat_routes.shape[0]
    onehot = (flat_routes[:, None] == jnp.arange(experts, dtype=jnp.int32)[None, :]).astype(
        jnp.int32
    )
    before = jnp.cumsum(onehot, axis=0) - onehot
    rank_in_expert = jnp.sum(before * onehot, axis=1)
    slot_of_pair = flat_routes * capacity + rank_in_expert
    pair_of_slot = (
        jnp.zeros((experts * capacity,), jnp.int32)
        .at[slot_of_pair]
        .set(jnp.arange(pair_count, dtype=jnp.int32))
    )
    filled = jnp.zeros((experts * capacity,), jnp.int32).at[slot_of_pair].set(1)
    return (slot_of_pair, pair_of_slot, filled)


def col_rows(block_array):
    return lax.all_gather(block_array, "col", axis=0, tiled=True)


def row_rows(block_array):
    return lax.all_gather(block_array, "row", axis=0, tiled=True)


def row_terms(term_maker, local_rows):
    return lax.psum_scatter(
        term_maker(jnp.int32(0), local_rows * lax.axis_size("row")),
        "row",
        scatter_dimension=0,
        tiled=True,
    )


def col_terms(term_maker, local_rows):
    return lax.psum_scatter(
        term_maker(jnp.int32(0), local_rows * lax.axis_size("col")),
        "col",
        scatter_dimension=0,
        tiled=True,
    )


def row_total(partial_sum):
    return lax.psum(partial_sum, "row")


def slicer(full_array):

    def take_rows(first_row, row_count):
        return full_array

    return take_rows


def per_device(
    block_input, attn_gain, w_qkv, w_out, ffn_gain, w_router, w_gate, w_up, w_down, routes, out_grad
):
    tok_local, width_local = block_input.shape
    model_width = width_local * lax.axis_size("row")
    seq_len = routes.shape[0]
    top_count = routes.shape[1]
    experts = w_gate.shape[0]
    ffn_local = w_gate.shape[2]
    capacity = CAP
    repeat = HEADS // KV_HEADS
    groups_local = KV_HEADS // lax.axis_size("col")
    kv_cols = groups_local * HEAD_DIM
    query_len = seq_len // lax.axis_size("row")
    slots_local = experts * capacity // lax.axis_size("row")
    row_index = lax.axis_index("row")
    col_index = lax.axis_index("col")
    score_scale = HEAD_DIM ** (-0.5)
    inputs_f = block_input.astype(jnp.float32)
    square_one = row_total(jnp.sum(inputs_f * inputs_f, axis=1))
    inv_rms_one = lax.rsqrt(square_one / model_width + epsilon)[:, None]
    unit_one = inputs_f * inv_rms_one
    normed_one = (unit_one * attn_gain).astype(jnp.bfloat16)
    normed_all = col_rows(normed_one)

    def qkv_term(first_row, row_count):
        return jnp.dot(normed_all, w_qkv, preferred_element_type=jnp.float32)

    proj_qkv = row_terms(qkv_term, query_len).reshape(query_len, groups_local, repeat + 2, HEAD_DIM)
    positions = row_index * query_len + jnp.arange(query_len, dtype=jnp.int32)
    cos_table, sin_table = rope_tables(positions, HEAD_DIM)
    queries = proj_qkv[:, :, :repeat]
    keys_raw = proj_qkv[:, :, repeat]
    vals_raw = proj_qkv[:, :, repeat + 1]
    queries_rot = (
        (queries * cos_table[:, None, None] + rotate_half(queries) * sin_table[:, None, None])
        * score_scale
    ).astype(jnp.bfloat16)
    keys_rot = (keys_raw * cos_table[:, None] + rotate_half(keys_raw) * sin_table[:, None]).astype(
        jnp.bfloat16
    )
    key_value = jnp.concatenate(
        [
            keys_rot.reshape(query_len, kv_cols),
            vals_raw.astype(jnp.bfloat16).reshape(query_len, kv_cols),
        ],
        axis=1,
    )
    key_value_all = row_rows(key_value)
    keys_all = key_value_all[:, :kv_cols].reshape(seq_len, groups_local, HEAD_DIM)
    values_all = key_value_all[:, kv_cols:].reshape(seq_len, groups_local, HEAD_DIM)
    causal = jnp.arange(seq_len, dtype=jnp.int32)[None, :] <= positions[:, None]
    scores = jnp.einsum("qgrd,kgd->grqk", queries_rot, keys_all, preferred_element_type=jnp.float32)
    exp_scores = jnp.where(causal, jnp.exp(scores), 0.0)
    log_total = jnp.log(jnp.sum(exp_scores, axis=-1, keepdims=True))
    attn_probs = jnp.where(causal, jnp.exp(scores - log_total), 0.0)
    probs_b = attn_probs.astype(jnp.bfloat16)
    attended = (
        jnp.einsum("grqk,kgd->qgrd", probs_b, values_all, preferred_element_type=jnp.float32)
        .astype(jnp.bfloat16)
        .reshape(query_len, -1)
    )
    attended_all = row_rows(attended)

    def attn_term(first_row, row_count):
        return jnp.dot(attended_all, w_out, preferred_element_type=jnp.float32)

    hidden_res = inputs_f + col_terms(attn_term, tok_local)
    gained = hidden_res * ffn_gain
    square_two, router_part = lax.psum(
        (
            jnp.sum(hidden_res * hidden_res, axis=1),
            jnp.dot(gained, w_router, precision=lax.Precision.HIGHEST),
        ),
        "row",
    )
    inv_rms_two = lax.rsqrt(square_two / model_width + epsilon)[:, None]
    unit_two = hidden_res * inv_rms_two
    normed_two_f = gained * inv_rms_two
    normed_two = normed_two_f.astype(jnp.bfloat16)
    logits = router_part * inv_rms_two
    routes_local = lax.dynamic_slice_in_dim(routes, col_index * tok_local, tok_local, 0)
    chosen_mask = (
        routes_local[:, :, None] == jnp.arange(experts, dtype=jnp.int32)[None, None, :]
    ).astype(jnp.float32)
    chosen = jnp.sum(chosen_mask * logits[:, None, :], axis=2)
    exp_chosen = jnp.exp(chosen)
    gate_weights = exp_chosen / jnp.sum(exp_chosen, axis=1, keepdims=True)
    normed_two_all = col_rows(normed_two)
    slot_of_pair, pair_of_slot, filled = slot_tables(routes, experts, capacity)
    token_of_slot = pair_of_slot // top_count
    slot_rows = jnp.where(filled[:, None] > 0, normed_two_all[token_of_slot], 0)
    w_both = jnp.concatenate([w_gate, w_up], axis=2)
    row_block = slot_rows.reshape(
        slots_local * lax.axis_size("row") // capacity, capacity, width_local
    )
    pre_act = lax.psum_scatter(
        jnp.einsum("ecd,edf->ecf", row_block, w_both, preferred_element_type=jnp.float32).reshape(
            slots_local * lax.axis_size("row"), 2 * ffn_local
        ),
        "row",
        scatter_dimension=0,
        tiled=True,
    )
    gate_pre = pre_act[:, :ffn_local]
    up_val = pre_act[:, ffn_local:]
    sigmoid_gate = jax.nn.sigmoid(gate_pre)
    activated = (gate_pre * sigmoid_gate * up_val).astype(jnp.bfloat16)
    activated_all = row_rows(activated)
    down_slots = jnp.einsum(
        "ecf,efd->ecd",
        activated_all.reshape(experts, capacity, ffn_local),
        w_down,
        preferred_element_type=jnp.float32,
    ).reshape(experts * capacity, width_local)
    pair_out = down_slots[slot_of_pair]
    pair_local = col_terms(slicer(pair_out), tok_local * top_count).reshape(
        tok_local, top_count, width_local
    )
    block_output = (hidden_res + jnp.sum(gate_weights[:, :, None] * pair_local, axis=1)).astype(
        jnp.bfloat16
    )
    grad_f = out_grad.astype(jnp.float32)
    gate_grads = row_total(jnp.sum(grad_f[:, None, :] * pair_local, axis=2))
    gate_mix = gate_weights * (
        gate_grads - jnp.sum(gate_weights * gate_grads, axis=1, keepdims=True)
    )
    logit_grads = jnp.sum(gate_mix[:, :, None] * chosen_mask, axis=1)
    pair_grad = (
        (gate_weights[:, :, None] * grad_f[:, None, :])
        .astype(jnp.bfloat16)
        .reshape(tok_local * top_count, width_local)
    )
    pair_grad_all = col_rows(pair_grad)
    slot_grad = jnp.where(filled[:, None] > 0, pair_grad_all[pair_of_slot], 0)

    def act_term(first_row, row_count):
        row_block = slot_grad.reshape(row_count // capacity, capacity, width_local)
        return jnp.einsum(
            "ecd,efd->ecf", row_block, w_down, preferred_element_type=jnp.float32
        ).reshape(row_count, ffn_local)

    act_grad = row_terms(act_term, slots_local)
    gate_pre_grad = act_grad * up_val * sigmoid_gate * (1.0 + gate_pre * (1.0 - sigmoid_gate))
    up_grad = act_grad * gate_pre * sigmoid_gate
    pre_grad = jnp.concatenate([gate_pre_grad, up_grad], axis=1).astype(jnp.bfloat16)
    pre_grad_all = row_rows(pre_grad).reshape(experts, capacity, 2 * ffn_local)
    down_grad = jnp.einsum(
        "ecf,ecd->efd",
        activated_all.reshape(experts, capacity, ffn_local),
        slot_grad.reshape(experts, capacity, width_local),
        preferred_element_type=jnp.float32,
    )
    both_grad = jnp.einsum(
        "ecd,ecf->edf",
        slot_rows.reshape(experts, capacity, width_local),
        pre_grad_all,
        preferred_element_type=jnp.float32,
    )
    slot_back = jnp.einsum(
        "ecf,edf->ecd", pre_grad_all, w_both, preferred_element_type=jnp.float32
    ).reshape(experts * capacity, width_local)
    token_back = jnp.sum(slot_back[slot_of_pair].reshape(seq_len, top_count, width_local), axis=1)
    normed_grad = col_terms(slicer(token_back), tok_local)
    normed_grad = normed_grad + jnp.dot(logit_grads, w_router.T, precision=lax.Precision.HIGHEST)
    ffn_gain_part = jnp.sum(normed_grad * unit_two, axis=0)
    router_part_grad = jnp.dot(normed_two_f.T, logit_grads, precision=lax.Precision.HIGHEST)
    unit_grad_two = normed_grad * ffn_gain
    inner_two = row_total(jnp.sum(unit_grad_two * unit_two, axis=1))
    residual_grad = grad_f + inv_rms_two * (
        unit_grad_two - unit_two * (inner_two / model_width)[:, None]
    )
    residual_b = residual_grad.astype(jnp.bfloat16)
    residual_all = col_rows(residual_b)
    out_proj_grad = jnp.einsum(
        "th,td->hd", attended_all, residual_all, preferred_element_type=jnp.float32
    )

    def attn_back_term(first_row, row_count):
        return jnp.einsum("td,hd->th", residual_all, w_out, preferred_element_type=jnp.float32)

    attended_grad = (
        row_terms(attn_back_term, query_len)
        .astype(jnp.bfloat16)
        .reshape(query_len, groups_local, repeat, HEAD_DIM)
    )
    prob_grad = jnp.einsum(
        "qgrd,kgd->grqk", attended_grad, values_all, preferred_element_type=jnp.float32
    )
    prob_inner = jnp.sum(attn_probs * prob_grad, axis=-1, keepdims=True)
    score_grad = (attn_probs * (prob_grad - prob_inner)).astype(jnp.bfloat16)
    query_grad = jnp.einsum(
        "grqk,kgd->qgrd", score_grad, keys_all, preferred_element_type=jnp.float32
    )
    key_part = jnp.einsum(
        "grqk,qgrd->kgd", score_grad, queries_rot, preferred_element_type=jnp.float32
    )
    value_part = jnp.einsum(
        "grqk,qgrd->kgd", probs_b, attended_grad, preferred_element_type=jnp.float32
    )
    kv_part = jnp.concatenate(
        [key_part.reshape(seq_len, kv_cols), value_part.reshape(seq_len, kv_cols)], axis=1
    )
    kv_grad = row_terms(slicer(kv_part), query_len)
    key_grad = kv_grad[:, :kv_cols].reshape(query_len, groups_local, HEAD_DIM)
    value_grad = kv_grad[:, kv_cols:].reshape(query_len, groups_local, HEAD_DIM)
    query_back = (
        query_grad * cos_table[:, None, None] - rotate_half(query_grad * sin_table[:, None, None])
    ) * score_scale
    key_back = key_grad * cos_table[:, None] - rotate_half(key_grad * sin_table[:, None])
    qkv_grad = (
        jnp.concatenate([query_back, key_back[:, :, None], value_grad[:, :, None]], axis=2)
        .reshape(query_len, -1)
        .astype(jnp.bfloat16)
    )
    qkv_grad_all = row_rows(qkv_grad)
    qkv_weight_part = jnp.einsum(
        "td,tc->dc", normed_all, qkv_grad_all, preferred_element_type=jnp.float32
    )

    def norm_back_term(first_row, row_count):
        return jnp.einsum("tc,dc->td", qkv_grad_all, w_qkv, preferred_element_type=jnp.float32)

    normed_one_grad = col_terms(norm_back_term, tok_local)
    attn_gain_part = jnp.sum(normed_one_grad * unit_one, axis=0)
    unit_grad_one = normed_one_grad * attn_gain
    inner_one = row_total(jnp.sum(unit_grad_one * unit_one, axis=1))
    input_grad = residual_grad + inv_rms_one * (
        unit_grad_one - unit_one * (inner_one / model_width)[:, None]
    )
    grad_qkv, grad_out = (
        lax.psum(qkv_weight_part.astype(jnp.bfloat16), "dp").astype(jnp.float32),
        lax.psum(out_proj_grad.astype(jnp.bfloat16), "dp").astype(jnp.float32),
    )
    grad_attn_gain, grad_ffn_gain, grad_router = lax.psum(
        (attn_gain_part, ffn_gain_part, router_part_grad), ("dp", "col")
    )
    grad_gate, grad_up, grad_down = (
        lax.psum_scatter(
            both_grad[:, :, :ffn_local].astype(jnp.bfloat16), "dp", scatter_dimension=0, tiled=True
        ).astype(jnp.float32),
        lax.psum_scatter(
            both_grad[:, :, ffn_local:].astype(jnp.bfloat16), "dp", scatter_dimension=0, tiled=True
        ).astype(jnp.float32),
        lax.psum_scatter(
            down_grad.astype(jnp.bfloat16), "dp", scatter_dimension=0, tiled=True
        ).astype(jnp.float32),
    )
    return (
        block_output,
        input_grad,
        grad_attn_gain,
        grad_qkv,
        grad_out,
        grad_ffn_gain,
        grad_router,
        grad_gate,
        grad_up,
        grad_down,
    )


def from_blocks(blocks):
    row_blocks, col_blocks, height, width = blocks.shape
    return blocks.transpose(0, 2, 1, 3).reshape(row_blocks * height, col_blocks * width)


def to_blocks(full_array, height, width):
    rows, cols = full_array.shape
    return full_array.reshape(rows // height, height, cols // width, width).transpose(0, 2, 1, 3)


def expert_owner(
    block_input, attn_gain, w_qkv, w_out, ffn_gain, w_router, w_gate, w_up, w_down, routes, out_grad
):
    tok_local, width_local = block_input.shape
    dp_size, row_size, col_size = (lax.axis_size(name) for name in ("dp", "row", "col"))
    model_width = width_local * row_size
    seq_len = routes.shape[0]
    tokens = seq_len * dp_size
    experts = w_gate.shape[0]
    ffn_local = w_gate.shape[2]
    ffn = ffn_local * col_size
    repeat = HEADS // KV_HEADS
    groups_local = KV_HEADS // col_size
    head_cols = groups_local * repeat * HEAD_DIM
    dp_index, row_index, col_index = (lax.axis_index(name) for name in ("dp", "row", "col"))
    score_scale = HEAD_DIM ** (-0.5)
    everyone = ("dp", "col", "row")
    peers = ("row", "col")
    owned = experts // dp_size
    own_expert = dp_index * owned + row_index * col_size + col_index
    token_blocks = dp_size * col_size
    tok_share = tokens // (token_blocks * row_size)
    seq_first = dp_index * seq_len
    block_first = (dp_index * col_size + col_index) * tok_local
    share_first = block_first + row_index * tok_share
    width_first = row_index * width_local

    def rows_of(full_array, first_row, count):
        return lax.dynamic_slice_in_dim(full_array, first_row, count, 0)

    def cols_of(full_array, first_col, count):
        return lax.dynamic_slice_in_dim(full_array, first_col, count, 1)

    def whole(block_array):
        gathered = lax.all_gather(block_array, everyone, axis=0)
        return from_blocks(gathered.reshape(token_blocks, row_size, tok_local, width_local))

    inputs_f = whole(block_input).astype(jnp.float32)
    w_qkv_all = lax.all_gather(w_qkv, "row", axis=0, tiled=True)
    small = jnp.concatenate([w_router, attn_gain[:, None], ffn_gain[:, None]], axis=1)
    small_all = lax.all_gather(small, "row", axis=0, tiled=True)
    w_router_all = small_all[:, :experts]
    attn_gain_all = small_all[:, experts]
    ffn_gain_all = small_all[:, experts + 1]
    routes_all = lax.all_gather(routes, "dp", axis=0, tiled=True)
    w_out_all = from_blocks(
        lax.all_gather(w_out, ("col", "row"), axis=0).reshape(
            col_size, row_size, w_out.shape[0], width_local
        )
    )
    grad_f = whole(out_grad).astype(jnp.float32)

    def own_weight(weight):
        mine = lax.dynamic_slice_in_dim(weight, dp_index * owned, owned, 0)
        moved = lax.all_to_all(mine, peers, 0, 0, tiled=True)
        return moved.reshape((row_size, col_size) + weight.shape[1:])

    gate_own = from_blocks(own_weight(w_gate))
    up_own = from_blocks(own_weight(w_up))
    down_own = from_blocks(own_weight(w_down).transpose(1, 0, 2, 3))

    inv_rms_one = lax.rsqrt(jnp.mean(inputs_f * inputs_f, axis=1, keepdims=True) + epsilon)
    unit_one = inputs_f * inv_rms_one
    normed_one = (unit_one * attn_gain_all).astype(jnp.bfloat16)
    normed_seq = rows_of(normed_one, seq_first, seq_len)
    proj_flat = jnp.dot(normed_seq, w_qkv_all, preferred_element_type=jnp.float32)
    proj_qkv = proj_flat.reshape(seq_len, groups_local, repeat + 2, HEAD_DIM)
    positions = jnp.arange(seq_len, dtype=jnp.int32)
    cos_table, sin_table = rope_tables(positions, HEAD_DIM)
    queries = proj_qkv[:, :, :repeat]
    keys_raw = proj_qkv[:, :, repeat]
    values_all = proj_qkv[:, :, repeat + 1].astype(jnp.bfloat16)
    queries_rot = (
        (queries * cos_table[:, None, None] + rotate_half(queries) * sin_table[:, None, None])
        * score_scale
    ).astype(jnp.bfloat16)
    keys_all = (keys_raw * cos_table[:, None] + rotate_half(keys_raw) * sin_table[:, None]).astype(
        jnp.bfloat16
    )
    causal = positions[None, :] <= positions[:, None]
    scores = jnp.einsum("qgrd,kgd->grqk", queries_rot, keys_all, preferred_element_type=jnp.float32)
    exp_scores = jnp.where(causal, jnp.exp(scores), 0.0)
    log_total = jnp.log(jnp.sum(exp_scores, axis=-1, keepdims=True))
    attn_probs = jnp.where(causal, jnp.exp(scores - log_total), 0.0)
    probs_b = attn_probs.astype(jnp.bfloat16)
    attended = (
        jnp.einsum("grqk,kgd->qgrd", probs_b, values_all, preferred_element_type=jnp.float32)
        .astype(jnp.bfloat16)
        .reshape(seq_len, head_cols)
    )
    attended_all = from_blocks(
        lax.all_gather(attended, ("dp", "col"), axis=0).reshape(
            dp_size, col_size, seq_len, head_cols
        )
    )
    hidden_res = inputs_f + jnp.dot(attended_all, w_out_all, preferred_element_type=jnp.float32)
    inv_rms_two = lax.rsqrt(jnp.mean(hidden_res * hidden_res, axis=1, keepdims=True) + epsilon)
    unit_two = hidden_res * inv_rms_two
    normed_two_f = unit_two * ffn_gain_all
    normed_two = normed_two_f.astype(jnp.bfloat16)
    logits = jnp.dot(normed_two_f, w_router_all, precision=lax.Precision.HIGHEST)
    chosen_mask = jnp.any(
        routes_all[:, :, None] == jnp.arange(experts, dtype=jnp.int32)[None, None, :], axis=1
    )
    exp_chosen = jnp.where(chosen_mask, jnp.exp(logits), 0.0)
    gate_weights = exp_chosen / jnp.sum(exp_chosen, axis=1, keepdims=True)
    gate_own_weight = cols_of(gate_weights, own_expert, 1)

    gate_pre = jnp.dot(normed_two, gate_own, preferred_element_type=jnp.float32)
    up_val = jnp.dot(normed_two, up_own, preferred_element_type=jnp.float32)
    sigmoid_gate = jax.nn.sigmoid(gate_pre)
    activated = (gate_pre * sigmoid_gate * up_val).astype(jnp.bfloat16)
    pair_out = jnp.dot(activated, down_own, preferred_element_type=jnp.float32)
    gate_grads = lax.all_gather(
        jnp.sum(grad_f * pair_out, axis=1), ("dp", "row", "col"), axis=0
    ).T
    gate_mix = gate_weights * (
        gate_grads - jnp.sum(gate_weights * gate_grads, axis=1, keepdims=True)
    )
    pair_grad = (gate_own_weight * grad_f).astype(jnp.bfloat16)
    act_grad = lax.dot_general(
        pair_grad, down_own, (((1,), (1,)), ((), ())), preferred_element_type=jnp.float32
    )
    gate_pre_grad = (
        act_grad * up_val * sigmoid_gate * (1.0 + gate_pre * (1.0 - sigmoid_gate))
    ).astype(jnp.bfloat16)
    up_grad = (act_grad * gate_pre * sigmoid_gate).astype(jnp.bfloat16)
    token_back = lax.dot_general(
        gate_pre_grad, gate_own, (((1,), (1,)), ((), ())), preferred_element_type=jnp.float32
    ) + lax.dot_general(
        up_grad, up_own, (((1,), (1,)), ((), ())), preferred_element_type=jnp.float32
    )
    back_share = lax.psum_scatter(
        token_back.astype(jnp.bfloat16), everyone, scatter_dimension=0, tiled=True
    ).astype(jnp.float32)
    moe_block = lax.psum_scatter(
        to_blocks(
            (gate_own_weight * pair_out).astype(jnp.bfloat16), tok_local, width_local
        ).reshape(token_blocks * row_size, tok_local, width_local),
        everyone,
        scatter_dimension=0,
        tiled=True,
    ).reshape(tok_local, width_local)
    own_hidden = cols_of(rows_of(hidden_res, block_first, tok_local), width_first, width_local)
    block_output = (own_hidden + moe_block.astype(jnp.float32)).astype(jnp.bfloat16)

    normed_grad = back_share + jnp.dot(
        rows_of(gate_mix, share_first, tok_share), w_router_all.T, precision=lax.Precision.HIGHEST
    )
    unit_share = rows_of(unit_two, share_first, tok_share)
    ffn_gain_part = jnp.sum(normed_grad * unit_share, axis=0)
    unit_grad_two = normed_grad * ffn_gain_all
    residual_share = rows_of(grad_f, share_first, tok_share) + rows_of(
        inv_rms_two, share_first, tok_share
    ) * (unit_grad_two - unit_share * jnp.mean(unit_grad_two * unit_share, axis=1, keepdims=True))
    residual_all = lax.all_gather(
        residual_share.astype(jnp.bfloat16), everyone, axis=0, tiled=True
    )

    def expert_grad(blocks):
        return lax.all_to_all(blocks, peers, 0, 0, tiled=True).astype(jnp.float32)

    def turned(left, right):
        return lax.dot_general(
            left, right, (((0,), (0,)), ((), ())), preferred_element_type=jnp.float32
        )

    def sent(blocks):
        return blocks.reshape((row_size * col_size,) + blocks.shape[2:])

    grad_down = expert_grad(
        sent(
            to_blocks(
                turned(activated, pair_grad).astype(jnp.bfloat16), ffn_local, width_local
            ).transpose(1, 0, 2, 3)
        )
    )
    grad_gate = expert_grad(
        sent(to_blocks(turned(normed_two, gate_pre_grad).astype(jnp.bfloat16), width_local, ffn_local))
    )
    grad_up = expert_grad(
        sent(to_blocks(turned(normed_two, up_grad).astype(jnp.bfloat16), width_local, ffn_local))
    )
    grad_router = lax.dot_general(
        cols_of(normed_two_f, width_first, width_local),
        gate_mix,
        (((0,), (0,)), ((), ())),
        precision=lax.Precision.HIGHEST,
    )

    grad_out = turned(
        cols_of(attended_all, col_index * head_cols, head_cols),
        cols_of(residual_all, width_first, width_local),
    )
    attended_grad = (
        lax.dot_general(
            rows_of(residual_all, seq_first, seq_len),
            rows_of(w_out_all, col_index * head_cols, head_cols),
            (((1,), (1,)), ((), ())),
            preferred_element_type=jnp.float32,
        )
        .astype(jnp.bfloat16)
        .reshape(seq_len, groups_local, repeat, HEAD_DIM)
    )
    prob_grad = jnp.einsum(
        "qgrd,kgd->grqk", attended_grad, values_all, preferred_element_type=jnp.float32
    )
    prob_inner = jnp.sum(attn_probs * prob_grad, axis=-1, keepdims=True)
    score_grad = (attn_probs * (prob_grad - prob_inner)).astype(jnp.bfloat16)
    query_grad = jnp.einsum(
        "grqk,kgd->qgrd", score_grad, keys_all, preferred_element_type=jnp.float32
    )
    key_grad = jnp.einsum(
        "grqk,qgrd->kgd", score_grad, queries_rot, preferred_element_type=jnp.float32
    )
    value_grad = jnp.einsum(
        "grqk,qgrd->kgd", probs_b, attended_grad, preferred_element_type=jnp.float32
    )
    query_back = (
        query_grad * cos_table[:, None, None] - rotate_half(query_grad * sin_table[:, None, None])
    ) * score_scale
    key_back = key_grad * cos_table[:, None] - rotate_half(key_grad * sin_table[:, None])
    qkv_grad = (
        jnp.concatenate([query_back, key_back[:, :, None], value_grad[:, :, None]], axis=2)
        .reshape(seq_len, -1)
        .astype(jnp.bfloat16)
    )
    grad_qkv = lax.psum(
        turned(cols_of(normed_seq, width_first, width_local), qkv_grad).astype(jnp.bfloat16), "dp"
    ).astype(jnp.float32)
    norm_back = lax.dot_general(
        qkv_grad, w_qkv, (((1,), (1,)), ((), ())), preferred_element_type=jnp.float32
    )
    unit_own = cols_of(rows_of(unit_one, seq_first, seq_len), width_first, width_local)
    attn_gain_part = jnp.sum(norm_back * unit_own, axis=0)
    inner_part = jnp.sum(qkv_grad.astype(jnp.float32) * proj_flat, axis=1, keepdims=True)
    input_part = rows_of(inv_rms_one, seq_first, seq_len) * (
        norm_back * attn_gain - unit_own * (inner_part / model_width)
    )
    own_residual = cols_of(rows_of(residual_all, block_first, tok_local), width_first, width_local)
    input_grad = own_residual.astype(jnp.float32) + lax.psum_scatter(
        input_part, "col", scatter_dimension=0, tiled=True
    )
    attn_gain_wide = lax.dynamic_update_slice_in_dim(
        jnp.zeros((model_width,), jnp.float32), attn_gain_part, width_first, 0
    )
    gains = lax.psum(jnp.stack([attn_gain_wide, ffn_gain_part]), ("dp", "row", "col"))
    gains_own = cols_of(gains, width_first, width_local)
    return (
        block_output,
        input_grad,
        gains_own[0],
        grad_qkv,
        grad_out,
        gains_own[1],
        grad_router,
        grad_gate,
        grad_up,
        grad_down,
    )


def solution(mesh):
    in_specs = (
        P(("dp", "col"), "row"),
        P("row"),
        P("row", "col"),
        P("col", "row"),
        P("row"),
        P("row", None),
        P(None, "row", "col"),
        P(None, "row", "col"),
        P(None, "col", "row"),
        P("dp", None),
        P(("dp", "col"), "row"),
    )
    out_specs = (
        P(("dp", "col"), "row"),
        P(("dp", "col"), "row"),
        P("row"),
        P("row", "col"),
        P("col", "row"),
        P("row"),
        P("row", None),
        P("dp", "row", "col"),
        P("dp", "row", "col"),
        P("dp", "col", "row"),
    )
    sizes = dict(mesh.shape)
    one_expert_each = sizes["dp"] * sizes["row"] * sizes["col"] == EXPERTS
    return jax.shard_map(
        expert_owner if one_expert_each else per_device, mesh=mesh, in_specs=in_specs, out_specs=out_specs, check_vma=False
    )
```

```python
import jax
import jax.numpy as jnp
from jax import lax
from jax.sharding import PartitionSpec as P

HEADS = 16
KV_HEADS = 8
HEAD_DIM = 64
CAP = 192
EXPERTS = 32


epsilon = 1e-06
rope_base = 10000.0


def rotate_half(head_values):
    half_width = head_values.shape[-1] // 2
    return jnp.concatenate([-head_values[..., half_width:], head_values[..., :half_width]], axis=-1)


def rope_tables(positions, head_dim):
    half_width = head_dim // 2
    inverse = rope_base ** (-jnp.arange(half_width, dtype=jnp.float32) / half_width)
    angles = positions.astype(jnp.float32)[:, None] * inverse[None, :]
    cos_table = jnp.cos(angles)
    sin_table = jnp.sin(angles)
    return (
        jnp.concatenate([cos_table, cos_table], axis=-1),
        jnp.concatenate([sin_table, sin_table], axis=-1),
    )


def slot_tables(routes_seq, experts, capacity):
    flat_routes = routes_seq.reshape(-1)
    pair_count = flat_routes.shape[0]
    onehot = (flat_routes[:, None] == jnp.arange(experts, dtype=jnp.int32)[None, :]).astype(
        jnp.int32
    )
    before = jnp.cumsum(onehot, axis=0) - onehot
    rank_in_expert = jnp.sum(before * onehot, axis=1)
    slot_of_pair = flat_routes * capacity + rank_in_expert
    pair_of_slot = (
        jnp.zeros((experts * capacity,), jnp.int32)
        .at[slot_of_pair]
        .set(jnp.arange(pair_count, dtype=jnp.int32))
    )
    filled = jnp.zeros((experts * capacity,), jnp.int32).at[slot_of_pair].set(1)
    return (slot_of_pair, pair_of_slot, filled)


def col_rows(block_array):
    return lax.all_gather(block_array, "col", axis=0, tiled=True)


def row_rows(block_array):
    return lax.all_gather(block_array, "row", axis=0, tiled=True)


def row_terms(term_maker, local_rows):
    return lax.psum_scatter(
        term_maker(jnp.int32(0), local_rows * lax.axis_size("row")),
        "row",
        scatter_dimension=0,
        tiled=True,
    )


def col_terms(term_maker, local_rows):
    return lax.psum_scatter(
        term_maker(jnp.int32(0), local_rows * lax.axis_size("col")),
        "col",
        scatter_dimension=0,
        tiled=True,
    )


def row_total(partial_sum):
    return lax.psum(partial_sum, "row")


def slicer(full_array):

    def take_rows(first_row, row_count):
        return full_array

    return take_rows


def per_device(
    block_input, attn_gain, w_qkv, w_out, ffn_gain, w_router, w_gate, w_up, w_down, routes, out_grad
):
    tok_local, width_local = block_input.shape
    model_width = width_local * lax.axis_size("row")
    seq_len = routes.shape[0]
    top_count = routes.shape[1]
    experts = w_gate.shape[0]
    ffn_local = w_gate.shape[2]
    capacity = CAP
    repeat = HEADS // KV_HEADS
    groups_local = KV_HEADS // lax.axis_size("col")
    kv_cols = groups_local * HEAD_DIM
    query_len = seq_len // lax.axis_size("row")
    slots_local = experts * capacity // lax.axis_size("row")
    row_index = lax.axis_index("row")
    col_index = lax.axis_index("col")
    score_scale = HEAD_DIM ** (-0.5)
    inputs_f = block_input.astype(jnp.float32)
    square_one = row_total(jnp.sum(inputs_f * inputs_f, axis=1))
    inv_rms_one = lax.rsqrt(square_one / model_width + epsilon)[:, None]
    unit_one = inputs_f * inv_rms_one
    normed_one = (unit_one * attn_gain).astype(jnp.bfloat16)
    normed_all = col_rows(normed_one)

    def qkv_term(first_row, row_count):
        return jnp.dot(normed_all, w_qkv, preferred_element_type=jnp.float32)

    proj_qkv = row_terms(qkv_term, query_len).reshape(query_len, groups_local, repeat + 2, HEAD_DIM)
    positions = row_index * query_len + jnp.arange(query_len, dtype=jnp.int32)
    cos_table, sin_table = rope_tables(positions, HEAD_DIM)
    queries = proj_qkv[:, :, :repeat]
    keys_raw = proj_qkv[:, :, repeat]
    vals_raw = proj_qkv[:, :, repeat + 1]
    queries_rot = (
        (queries * cos_table[:, None, None] + rotate_half(queries) * sin_table[:, None, None])
        * score_scale
    ).astype(jnp.bfloat16)
    keys_rot = (keys_raw * cos_table[:, None] + rotate_half(keys_raw) * sin_table[:, None]).astype(
        jnp.bfloat16
    )
    key_value = jnp.concatenate(
        [
            keys_rot.reshape(query_len, kv_cols),
            vals_raw.astype(jnp.bfloat16).reshape(query_len, kv_cols),
        ],
        axis=1,
    )
    key_value_all = row_rows(key_value)
    keys_all = key_value_all[:, :kv_cols].reshape(seq_len, groups_local, HEAD_DIM)
    values_all = key_value_all[:, kv_cols:].reshape(seq_len, groups_local, HEAD_DIM)
    causal = jnp.arange(seq_len, dtype=jnp.int32)[None, :] <= positions[:, None]
    scores = jnp.einsum("qgrd,kgd->grqk", queries_rot, keys_all, preferred_element_type=jnp.float32)
    exp_scores = jnp.where(causal, jnp.exp(scores), 0.0)
    log_total = jnp.log(jnp.sum(exp_scores, axis=-1, keepdims=True))
    attn_probs = jnp.where(causal, jnp.exp(scores - log_total), 0.0)
    probs_b = attn_probs.astype(jnp.bfloat16)
    attended = (
        jnp.einsum("grqk,kgd->qgrd", probs_b, values_all, preferred_element_type=jnp.float32)
        .astype(jnp.bfloat16)
        .reshape(query_len, -1)
    )
    attended_all = row_rows(attended)

    def attn_term(first_row, row_count):
        return jnp.dot(attended_all, w_out, preferred_element_type=jnp.float32)

    hidden_res = inputs_f + col_terms(attn_term, tok_local)
    gained = hidden_res * ffn_gain
    square_two, router_part = lax.psum(
        (
            jnp.sum(hidden_res * hidden_res, axis=1),
            jnp.dot(gained, w_router, precision=lax.Precision.HIGHEST),
        ),
        "row",
    )
    inv_rms_two = lax.rsqrt(square_two / model_width + epsilon)[:, None]
    unit_two = hidden_res * inv_rms_two
    normed_two_f = gained * inv_rms_two
    normed_two = normed_two_f.astype(jnp.bfloat16)
    logits = router_part * inv_rms_two
    routes_local = lax.dynamic_slice_in_dim(routes, col_index * tok_local, tok_local, 0)
    chosen_mask = (
        routes_local[:, :, None] == jnp.arange(experts, dtype=jnp.int32)[None, None, :]
    ).astype(jnp.float32)
    chosen = jnp.sum(chosen_mask * logits[:, None, :], axis=2)
    exp_chosen = jnp.exp(chosen)
    gate_weights = exp_chosen / jnp.sum(exp_chosen, axis=1, keepdims=True)
    normed_two_all = col_rows(normed_two)
    slot_of_pair, pair_of_slot, filled = slot_tables(routes, experts, capacity)
    token_of_slot = pair_of_slot // top_count
    slot_rows = jnp.where(filled[:, None] > 0, normed_two_all[token_of_slot], 0)
    w_both = jnp.concatenate([w_gate, w_up], axis=2)
    row_block = slot_rows.reshape(
        slots_local * lax.axis_size("row") // capacity, capacity, width_local
    )
    pre_act = lax.psum_scatter(
        jnp.einsum("ecd,edf->ecf", row_block, w_both, preferred_element_type=jnp.float32).reshape(
            slots_local * lax.axis_size("row"), 2 * ffn_local
        ),
        "row",
        scatter_dimension=0,
        tiled=True,
    )
    gate_pre = pre_act[:, :ffn_local]
    up_val = pre_act[:, ffn_local:]
    sigmoid_gate = jax.nn.sigmoid(gate_pre)
    activated = (gate_pre * sigmoid_gate * up_val).astype(jnp.bfloat16)
    activated_all = row_rows(activated)
    down_slots = jnp.einsum(
        "ecf,efd->ecd",
        activated_all.reshape(experts, capacity, ffn_local),
        w_down,
        preferred_element_type=jnp.float32,
    ).reshape(experts * capacity, width_local)
    pair_out = down_slots[slot_of_pair]
    pair_local = col_terms(slicer(pair_out), tok_local * top_count).reshape(
        tok_local, top_count, width_local
    )
    block_output = (hidden_res + jnp.sum(gate_weights[:, :, None] * pair_local, axis=1)).astype(
        jnp.bfloat16
    )
    grad_f = out_grad.astype(jnp.float32)
    gate_grads = row_total(jnp.sum(grad_f[:, None, :] * pair_local, axis=2))
    gate_mix = gate_weights * (
        gate_grads - jnp.sum(gate_weights * gate_grads, axis=1, keepdims=True)
    )
    logit_grads = jnp.sum(gate_mix[:, :, None] * chosen_mask, axis=1)
    pair_grad = (
        (gate_weights[:, :, None] * grad_f[:, None, :])
        .astype(jnp.bfloat16)
        .reshape(tok_local * top_count, width_local)
    )
    pair_grad_all = col_rows(pair_grad)
    slot_grad = jnp.where(filled[:, None] > 0, pair_grad_all[pair_of_slot], 0)

    def act_term(first_row, row_count):
        row_block = slot_grad.reshape(row_count // capacity, capacity, width_local)
        return jnp.einsum(
            "ecd,efd->ecf", row_block, w_down, preferred_element_type=jnp.float32
        ).reshape(row_count, ffn_local)

    act_grad = row_terms(act_term, slots_local)
    gate_pre_grad = act_grad * up_val * sigmoid_gate * (1.0 + gate_pre * (1.0 - sigmoid_gate))
    up_grad = act_grad * gate_pre * sigmoid_gate
    pre_grad = jnp.concatenate([gate_pre_grad, up_grad], axis=1).astype(jnp.bfloat16)
    pre_grad_all = row_rows(pre_grad).reshape(experts, capacity, 2 * ffn_local)
    down_grad = jnp.einsum(
        "ecf,ecd->efd",
        activated_all.reshape(experts, capacity, ffn_local),
        slot_grad.reshape(experts, capacity, width_local),
        preferred_element_type=jnp.float32,
    )
    both_grad = jnp.einsum(
        "ecd,ecf->edf",
        slot_rows.reshape(experts, capacity, width_local),
        pre_grad_all,
        preferred_element_type=jnp.float32,
    )
    slot_back = jnp.einsum(
        "ecf,edf->ecd", pre_grad_all, w_both, preferred_element_type=jnp.float32
    ).reshape(experts * capacity, width_local)
    token_back = jnp.sum(slot_back[slot_of_pair].reshape(seq_len, top_count, width_local), axis=1)
    normed_grad = col_terms(slicer(token_back), tok_local)
    normed_grad = normed_grad + jnp.dot(logit_grads, w_router.T, precision=lax.Precision.HIGHEST)
    ffn_gain_part = jnp.sum(normed_grad * unit_two, axis=0)
    router_part_grad = jnp.dot(normed_two_f.T, logit_grads, precision=lax.Precision.HIGHEST)
    unit_grad_two = normed_grad * ffn_gain
    inner_two = row_total(jnp.sum(unit_grad_two * unit_two, axis=1))
    residual_grad = grad_f + inv_rms_two * (
        unit_grad_two - unit_two * (inner_two / model_width)[:, None]
    )
    residual_b = residual_grad.astype(jnp.bfloat16)
    residual_all = col_rows(residual_b)
    out_proj_grad = jnp.einsum(
        "th,td->hd", attended_all, residual_all, preferred_element_type=jnp.float32
    )

    def attn_back_term(first_row, row_count):
        return jnp.einsum("td,hd->th", residual_all, w_out, preferred_element_type=jnp.float32)

    attended_grad = (
        row_terms(attn_back_term, query_len)
        .astype(jnp.bfloat16)
        .reshape(query_len, groups_local, repeat, HEAD_DIM)
    )
    prob_grad = jnp.einsum(
        "qgrd,kgd->grqk", attended_grad, values_all, preferred_element_type=jnp.float32
    )
    prob_inner = jnp.sum(attn_probs * prob_grad, axis=-1, keepdims=True)
    score_grad = (attn_probs * (prob_grad - prob_inner)).astype(jnp.bfloat16)
    query_grad = jnp.einsum(
        "grqk,kgd->qgrd", score_grad, keys_all, preferred_element_type=jnp.float32
    )
    key_part = jnp.einsum(
        "grqk,qgrd->kgd", score_grad, queries_rot, preferred_element_type=jnp.float32
    )
    value_part = jnp.einsum(
        "grqk,qgrd->kgd", probs_b, attended_grad, preferred_element_type=jnp.float32
    )
    kv_part = jnp.concatenate(
        [key_part.reshape(seq_len, kv_cols), value_part.reshape(seq_len, kv_cols)], axis=1
    )
    kv_grad = row_terms(slicer(kv_part), query_len)
    key_grad = kv_grad[:, :kv_cols].reshape(query_len, groups_local, HEAD_DIM)
    value_grad = kv_grad[:, kv_cols:].reshape(query_len, groups_local, HEAD_DIM)
    query_back = (
        query_grad * cos_table[:, None, None] - rotate_half(query_grad * sin_table[:, None, None])
    ) * score_scale
    key_back = key_grad * cos_table[:, None] - rotate_half(key_grad * sin_table[:, None])
    qkv_grad = (
        jnp.concatenate([query_back, key_back[:, :, None], value_grad[:, :, None]], axis=2)
        .reshape(query_len, -1)
        .astype(jnp.bfloat16)
    )
    qkv_grad_all = row_rows(qkv_grad)
    qkv_weight_part = jnp.einsum(
        "td,tc->dc", normed_all, qkv_grad_all, preferred_element_type=jnp.float32
    )

    def norm_back_term(first_row, row_count):
        return jnp.einsum("tc,dc->td", qkv_grad_all, w_qkv, preferred_element_type=jnp.float32)

    normed_one_grad = col_terms(norm_back_term, tok_local)
    attn_gain_part = jnp.sum(normed_one_grad * unit_one, axis=0)
    unit_grad_one = normed_one_grad * attn_gain
    inner_one = row_total(jnp.sum(unit_grad_one * unit_one, axis=1))
    input_grad = residual_grad + inv_rms_one * (
        unit_grad_one - unit_one * (inner_one / model_width)[:, None]
    )
    grad_qkv, grad_out = (
        lax.psum(qkv_weight_part.astype(jnp.bfloat16), "dp").astype(jnp.float32),
        lax.psum(out_proj_grad.astype(jnp.bfloat16), "dp").astype(jnp.float32),
    )
    grad_attn_gain, grad_ffn_gain, grad_router = lax.psum(
        (attn_gain_part, ffn_gain_part, router_part_grad), ("dp", "col")
    )
    grad_gate, grad_up, grad_down = (
        lax.psum_scatter(
            both_grad[:, :, :ffn_local].astype(jnp.bfloat16), "dp", scatter_dimension=0, tiled=True
        ).astype(jnp.float32),
        lax.psum_scatter(
            both_grad[:, :, ffn_local:].astype(jnp.bfloat16), "dp", scatter_dimension=0, tiled=True
        ).astype(jnp.float32),
        lax.psum_scatter(
            down_grad.astype(jnp.bfloat16), "dp", scatter_dimension=0, tiled=True
        ).astype(jnp.float32),
    )
    return (
        block_output,
        input_grad,
        grad_attn_gain,
        grad_qkv,
        grad_out,
        grad_ffn_gain,
        grad_router,
        grad_gate,
        grad_up,
        grad_down,
    )


def from_blocks(blocks):
    row_blocks, col_blocks, height, width = blocks.shape
    return blocks.transpose(0, 2, 1, 3).reshape(row_blocks * height, col_blocks * width)


def to_blocks(full_array, height, width):
    rows, cols = full_array.shape
    return full_array.reshape(rows // height, height, cols // width, width).transpose(0, 2, 1, 3)


def expert_owner(
    block_input, attn_gain, w_qkv, w_out, ffn_gain, w_router, w_gate, w_up, w_down, routes, out_grad
):
    tok_local, width_local = block_input.shape
    dp_size, row_size, col_size = (lax.axis_size(name) for name in ("dp", "row", "col"))
    model_width = width_local * row_size
    seq_len = routes.shape[0]
    tokens = seq_len * dp_size
    experts = w_gate.shape[0]
    ffn_local = w_gate.shape[2]
    ffn = ffn_local * col_size
    repeat = HEADS // KV_HEADS
    groups_local = KV_HEADS // col_size
    head_cols = groups_local * repeat * HEAD_DIM
    dp_index, row_index, col_index = (lax.axis_index(name) for name in ("dp", "row", "col"))
    score_scale = HEAD_DIM ** (-0.5)
    everyone = ("dp", "col", "row")
    peers = ("row", "col")
    owned = experts // dp_size
    own_expert = dp_index * owned + row_index * col_size + col_index
    token_blocks = dp_size * col_size
    tok_share = tokens // (token_blocks * row_size)
    seq_first = dp_index * seq_len
    block_first = (dp_index * col_size + col_index) * tok_local
    share_first = block_first + row_index * tok_share
    width_first = row_index * width_local

    def rows_of(full_array, first_row, count):
        return lax.dynamic_slice_in_dim(full_array, first_row, count, 0)

    def cols_of(full_array, first_col, count):
        return lax.dynamic_slice_in_dim(full_array, first_col, count, 1)

    def after(first, later):
        return lax.optimization_barrier((first, later))[1]

    def swap(blocks, names):
        return lax.all_to_all(blocks, names, 0, 0, tiled=True)

    def to_all(block_array, names, count):
        return swap(jnp.broadcast_to(block_array, (count,) + block_array.shape), names)

    def to_blocks_all(block_array):
        sent_on = to_all(block_array, ("dp", "col"), token_blocks)
        return sent_on.reshape(tokens, block_array.shape[1])

    def summed(blocks, names):
        return jnp.sum(swap(blocks, names).astype(jnp.float32), axis=0)

    def block_sum(full_array):
        blocks = full_array.reshape(token_blocks, tok_local, model_width)
        return summed(blocks, ("dp", "col")).astype(jnp.bfloat16)

    small = jnp.concatenate([w_router.T, attn_gain[None], ffn_gain[None]], axis=0)
    small_all = to_all(small, "row", row_size).transpose(1, 0, 2).reshape(-1, model_width)
    wide_input = to_all(block_input, "row", row_size).transpose(1, 0, 2)
    inputs_all = to_blocks_all(wide_input.reshape(tok_local, model_width))
    inputs_f = inputs_all.astype(jnp.float32)
    w_qkv_all = lax.all_gather(w_qkv, "row", axis=0, tiled=True)
    w_router_all = small_all[:experts].T
    attn_gain_all = small_all[experts]
    ffn_gain_all = small_all[experts + 1]
    routes_all = lax.all_gather(routes, "dp", axis=0, tiled=True)
    w_out_all = from_blocks(
        lax.all_gather(after(w_qkv_all, w_out), ("col", "row"), axis=0).reshape(
            col_size, row_size, w_out.shape[0], width_local
        )
    )
    grad_f = from_blocks(
        lax.all_gather(after(w_out_all, out_grad), everyone, axis=0).reshape(
            token_blocks, row_size, tok_local, width_local
        )
    ).astype(jnp.float32)

    def own_weight(weight):
        mine = lax.dynamic_slice_in_dim(weight, dp_index * owned, owned, 0)
        mine = after(inputs_all, mine)
        moved = lax.all_to_all(mine, peers, 0, 0, tiled=True)
        return moved.reshape((row_size, col_size) + weight.shape[1:])

    gate_own = from_blocks(own_weight(w_gate))
    up_own = from_blocks(own_weight(w_up))
    down_own = from_blocks(own_weight(w_down).transpose(1, 0, 2, 3))

    inv_rms_one = lax.rsqrt(jnp.mean(inputs_f * inputs_f, axis=1, keepdims=True) + epsilon)
    unit_one = inputs_f * inv_rms_one
    normed_one = (unit_one * attn_gain_all).astype(jnp.bfloat16)
    normed_seq = rows_of(normed_one, seq_first, seq_len)
    proj_flat = jnp.dot(normed_seq, w_qkv_all, preferred_element_type=jnp.float32)
    proj_qkv = proj_flat.reshape(seq_len, groups_local, repeat + 2, HEAD_DIM)
    positions = jnp.arange(seq_len, dtype=jnp.int32)
    cos_table, sin_table = rope_tables(positions, HEAD_DIM)
    queries = proj_qkv[:, :, :repeat]
    keys_raw = proj_qkv[:, :, repeat]
    values_all = proj_qkv[:, :, repeat + 1].astype(jnp.bfloat16)
    queries_rot = (
        (queries * cos_table[:, None, None] + rotate_half(queries) * sin_table[:, None, None])
        * score_scale
    ).astype(jnp.bfloat16)
    keys_all = (keys_raw * cos_table[:, None] + rotate_half(keys_raw) * sin_table[:, None]).astype(
        jnp.bfloat16
    )
    causal = positions[None, :] <= positions[:, None]
    scores = jnp.einsum("qgrd,kgd->grqk", queries_rot, keys_all, preferred_element_type=jnp.float32)
    exp_scores = jnp.where(causal, jnp.exp(scores), 0.0)
    log_total = jnp.log(jnp.sum(exp_scores, axis=-1, keepdims=True))
    attn_probs = jnp.where(causal, jnp.exp(scores - log_total), 0.0)
    probs_b = attn_probs.astype(jnp.bfloat16)
    attended = (
        jnp.einsum("grqk,kgd->qgrd", probs_b, values_all, preferred_element_type=jnp.float32)
        .astype(jnp.bfloat16)
        .reshape(seq_len, head_cols)
    )
    attended_all = from_blocks(
        to_all(attended, ("dp", "col"), token_blocks).reshape(
            dp_size, col_size, seq_len, head_cols
        )
    )
    hidden_res = inputs_f + jnp.dot(attended_all, w_out_all, preferred_element_type=jnp.float32)
    inv_rms_two = lax.rsqrt(jnp.mean(hidden_res * hidden_res, axis=1, keepdims=True) + epsilon)
    unit_two = hidden_res * inv_rms_two
    normed_two_f = unit_two * ffn_gain_all
    normed_two = normed_two_f.astype(jnp.bfloat16)
    logits = jnp.dot(normed_two_f, w_router_all, precision=lax.Precision.HIGHEST)
    chosen_mask = jnp.any(
        routes_all[:, :, None] == jnp.arange(experts, dtype=jnp.int32)[None, None, :], axis=1
    )
    exp_chosen = jnp.where(chosen_mask, jnp.exp(logits), 0.0)
    gate_weights = exp_chosen / jnp.sum(exp_chosen, axis=1, keepdims=True)
    gate_own_weight = cols_of(gate_weights, own_expert, 1)

    gate_pre = jnp.dot(normed_two, gate_own, preferred_element_type=jnp.float32)
    up_val = jnp.dot(normed_two, up_own, preferred_element_type=jnp.float32)
    sigmoid_gate = jax.nn.sigmoid(gate_pre)
    activated = (gate_pre * sigmoid_gate * up_val).astype(jnp.bfloat16)
    pair_out = jnp.dot(activated, down_own, preferred_element_type=jnp.float32)
    gate_grads = to_all(
        jnp.sum(grad_f * pair_out, axis=1).reshape(-1, 128), ("dp", "row", "col"), experts
    ).reshape(experts, tokens).T
    gate_mix = gate_weights * (
        gate_grads - jnp.sum(gate_weights * gate_grads, axis=1, keepdims=True)
    )
    pair_grad = (gate_own_weight * grad_f).astype(jnp.bfloat16)
    act_grad = lax.dot_general(
        pair_grad, down_own, (((1,), (1,)), ((), ())), preferred_element_type=jnp.float32
    )
    gate_pre_grad = (
        act_grad * up_val * sigmoid_gate * (1.0 + gate_pre * (1.0 - sigmoid_gate))
    ).astype(jnp.bfloat16)
    up_grad = (act_grad * gate_pre * sigmoid_gate).astype(jnp.bfloat16)
    token_back = lax.dot_general(
        gate_pre_grad, gate_own, (((1,), (1,)), ((), ())), preferred_element_type=jnp.float32
    ) + lax.dot_general(
        up_grad, up_own, (((1,), (1,)), ((), ())), preferred_element_type=jnp.float32
    )
    back_block = block_sum(token_back.astype(jnp.bfloat16))
    back_share = summed(back_block.reshape(row_size, tok_share, model_width), "row")
    normed_grad = back_share + jnp.dot(
        rows_of(gate_mix, share_first, tok_share), w_router_all.T, precision=lax.Precision.HIGHEST
    )
    unit_share = rows_of(unit_two, share_first, tok_share)
    ffn_gain_part = jnp.sum(normed_grad * unit_share, axis=0)
    unit_grad_two = normed_grad * ffn_gain_all
    residual_share = rows_of(grad_f, share_first, tok_share) + rows_of(
        inv_rms_two, share_first, tok_share
    ) * (unit_grad_two - unit_share * jnp.mean(unit_grad_two * unit_share, axis=1, keepdims=True))
    residual_block = to_all(residual_share.astype(jnp.bfloat16), "row", row_size)
    residual_all = to_blocks_all(residual_block.reshape(tok_local, model_width))

    moe_block = block_sum(after(residual_all, (gate_own_weight * pair_out).astype(jnp.bfloat16)))
    moe_own = summed(
        moe_block.reshape(tok_local, row_size, width_local).transpose(1, 0, 2), "row"
    )
    own_hidden = cols_of(rows_of(hidden_res, block_first, tok_local), width_first, width_local)
    block_output = (own_hidden + moe_own).astype(jnp.bfloat16)

    def expert_grad(blocks):
        return swap(blocks, peers).astype(jnp.float32)

    def turned(left, right):
        return lax.dot_general(
            left, right, (((0,), (0,)), ((), ())), preferred_element_type=jnp.float32
        )

    def sent(blocks):
        return blocks.reshape((row_size * col_size,) + blocks.shape[2:])

    grad_down = expert_grad(
        sent(
            to_blocks(
                turned(activated, pair_grad).astype(jnp.bfloat16), ffn_local, width_local
            ).transpose(1, 0, 2, 3)
        )
    )
    grad_gate = expert_grad(
        sent(to_blocks(turned(normed_two, gate_pre_grad).astype(jnp.bfloat16), width_local, ffn_local))
    )
    grad_up = expert_grad(
        sent(to_blocks(turned(normed_two, up_grad).astype(jnp.bfloat16), width_local, ffn_local))
    )
    grad_router = lax.dot_general(
        cols_of(normed_two_f, width_first, width_local),
        gate_mix,
        (((0,), (0,)), ((), ())),
        precision=lax.Precision.HIGHEST,
    )

    grad_out = turned(
        cols_of(attended_all, col_index * head_cols, head_cols),
        cols_of(residual_all, width_first, width_local),
    )
    attended_grad = (
        lax.dot_general(
            rows_of(residual_all, seq_first, seq_len),
            rows_of(w_out_all, col_index * head_cols, head_cols),
            (((1,), (1,)), ((), ())),
            preferred_element_type=jnp.float32,
        )
        .astype(jnp.bfloat16)
        .reshape(seq_len, groups_local, repeat, HEAD_DIM)
    )
    prob_grad = jnp.einsum(
        "qgrd,kgd->grqk", attended_grad, values_all, preferred_element_type=jnp.float32
    )
    prob_inner = jnp.sum(attn_probs * prob_grad, axis=-1, keepdims=True)
    score_grad = (attn_probs * (prob_grad - prob_inner)).astype(jnp.bfloat16)
    query_grad = jnp.einsum(
        "grqk,kgd->qgrd", score_grad, keys_all, preferred_element_type=jnp.float32
    )
    key_grad = jnp.einsum(
        "grqk,qgrd->kgd", score_grad, queries_rot, preferred_element_type=jnp.float32
    )
    value_grad = jnp.einsum(
        "grqk,qgrd->kgd", probs_b, attended_grad, preferred_element_type=jnp.float32
    )
    query_back = (
        query_grad * cos_table[:, None, None] - rotate_half(query_grad * sin_table[:, None, None])
    ) * score_scale
    key_back = key_grad * cos_table[:, None] - rotate_half(key_grad * sin_table[:, None])
    qkv_grad = (
        jnp.concatenate([query_back, key_back[:, :, None], value_grad[:, :, None]], axis=2)
        .reshape(seq_len, -1)
        .astype(jnp.bfloat16)
    )
    qkv_part = turned(cols_of(normed_seq, width_first, width_local), qkv_grad)
    grad_qkv = jnp.sum(
        to_all(qkv_part.astype(jnp.bfloat16), "dp", dp_size).astype(jnp.float32), axis=0
    )
    norm_back = lax.dot_general(
        qkv_grad, w_qkv, (((1,), (1,)), ((), ())), preferred_element_type=jnp.float32
    )
    unit_own = cols_of(rows_of(unit_one, seq_first, seq_len), width_first, width_local)
    attn_gain_part = jnp.sum(norm_back * unit_own, axis=0)
    inner_part = jnp.sum(qkv_grad.astype(jnp.float32) * proj_flat, axis=1, keepdims=True)
    input_part = rows_of(inv_rms_one, seq_first, seq_len) * (
        norm_back * attn_gain - unit_own * (inner_part / model_width)
    )
    own_residual = cols_of(rows_of(residual_all, block_first, tok_local), width_first, width_local)
    input_grad = own_residual.astype(jnp.float32) + summed(
        input_part.astype(jnp.bfloat16).reshape(col_size, tok_local, width_local), "col"
    )
    attn_gain_wide = lax.dynamic_update_slice_in_dim(
        jnp.zeros((model_width,), jnp.float32), attn_gain_part, width_first, 0
    )
    gain_parts = jnp.stack([attn_gain_wide, ffn_gain_part]).reshape(2, row_size, width_local)
    gains_own = summed(
        jnp.broadcast_to(
            gain_parts.transpose(1, 0, 2)[None, :, None],
            (dp_size, row_size, col_size, 2, width_local),
        ).reshape(experts, 2, width_local),
        ("dp", "row", "col"),
    )
    return (
        block_output,
        input_grad,
        gains_own[0],
        grad_qkv,
        grad_out,
        gains_own[1],
        grad_router,
        grad_gate,
        grad_up,
        grad_down,
    )


def solution(mesh):
    in_specs = (
        P(("dp", "col"), "row"),
        P("row"),
        P("row", "col"),
        P("col", "row"),
        P("row"),
        P("row", None),
        P(None, "row", "col"),
        P(None, "row", "col"),
        P(None, "col", "row"),
        P("dp", None),
        P(("dp", "col"), "row"),
    )
    out_specs = (
        P(("dp", "col"), "row"),
        P(("dp", "col"), "row"),
        P("row"),
        P("row", "col"),
        P("col", "row"),
        P("row"),
        P("row", None),
        P("dp", "row", "col"),
        P("dp", "row", "col"),
        P("dp", "col", "row"),
    )
    sizes = dict(mesh.shape)
    one_expert_each = sizes["dp"] * sizes["row"] * sizes["col"] == EXPERTS
    return jax.shard_map(
        expert_owner if one_expert_each else per_device, mesh=mesh, in_specs=in_specs, out_specs=out_specs, check_vma=False
    )
```

```python
import jax
import jax.numpy as jnp
from jax import lax
from jax.sharding import PartitionSpec as P

HEADS = 16
KV_HEADS = 8
HEAD_DIM = 64
CAP = 192
EXPERTS = 32


epsilon = 1e-06
rope_base = 10000.0


def rotate_half(head_values):
    half_width = head_values.shape[-1] // 2
    return jnp.concatenate([-head_values[..., half_width:], head_values[..., :half_width]], axis=-1)


def rope_tables(positions, head_dim):
    half_width = head_dim // 2
    inverse = rope_base ** (-jnp.arange(half_width, dtype=jnp.float32) / half_width)
    angles = positions.astype(jnp.float32)[:, None] * inverse[None, :]
    cos_table = jnp.cos(angles)
    sin_table = jnp.sin(angles)
    return (
        jnp.concatenate([cos_table, cos_table], axis=-1),
        jnp.concatenate([sin_table, sin_table], axis=-1),
    )


def slot_tables(routes_seq, experts, capacity):
    flat_routes = routes_seq.reshape(-1)
    pair_count = flat_routes.shape[0]
    onehot = (flat_routes[:, None] == jnp.arange(experts, dtype=jnp.int32)[None, :]).astype(
        jnp.int32
    )
    before = jnp.cumsum(onehot, axis=0) - onehot
    rank_in_expert = jnp.sum(before * onehot, axis=1)
    slot_of_pair = flat_routes * capacity + rank_in_expert
    pair_of_slot = (
        jnp.zeros((experts * capacity,), jnp.int32)
        .at[slot_of_pair]
        .set(jnp.arange(pair_count, dtype=jnp.int32))
    )
    filled = jnp.zeros((experts * capacity,), jnp.int32).at[slot_of_pair].set(1)
    return (slot_of_pair, pair_of_slot, filled)


def col_rows(block_array):
    return lax.all_gather(block_array, "col", axis=0, tiled=True)


def row_rows(block_array):
    return lax.all_gather(block_array, "row", axis=0, tiled=True)


def row_terms(term_maker, local_rows):
    return lax.psum_scatter(
        term_maker(jnp.int32(0), local_rows * lax.axis_size("row")),
        "row",
        scatter_dimension=0,
        tiled=True,
    )


def col_terms(term_maker, local_rows):
    return lax.psum_scatter(
        term_maker(jnp.int32(0), local_rows * lax.axis_size("col")),
        "col",
        scatter_dimension=0,
        tiled=True,
    )


def row_total(partial_sum):
    return lax.psum(partial_sum, "row")


def slicer(full_array):

    def take_rows(first_row, row_count):
        return full_array

    return take_rows


def per_device(
    block_input, attn_gain, w_qkv, w_out, ffn_gain, w_router, w_gate, w_up, w_down, routes, out_grad
):
    tok_local, width_local = block_input.shape
    model_width = width_local * lax.axis_size("row")
    seq_len = routes.shape[0]
    top_count = routes.shape[1]
    experts = w_gate.shape[0]
    ffn_local = w_gate.shape[2]
    capacity = CAP
    repeat = HEADS // KV_HEADS
    groups_local = KV_HEADS // lax.axis_size("col")
    kv_cols = groups_local * HEAD_DIM
    query_len = seq_len // lax.axis_size("row")
    slots_local = experts * capacity // lax.axis_size("row")
    row_index = lax.axis_index("row")
    col_index = lax.axis_index("col")
    score_scale = HEAD_DIM ** (-0.5)
    inputs_f = block_input.astype(jnp.float32)
    square_one = row_total(jnp.sum(inputs_f * inputs_f, axis=1))
    inv_rms_one = lax.rsqrt(square_one / model_width + epsilon)[:, None]
    unit_one = inputs_f * inv_rms_one
    normed_one = (unit_one * attn_gain).astype(jnp.bfloat16)
    normed_all = col_rows(normed_one)

    def qkv_term(first_row, row_count):
        return jnp.dot(normed_all, w_qkv, preferred_element_type=jnp.float32)

    proj_qkv = row_terms(qkv_term, query_len).reshape(query_len, groups_local, repeat + 2, HEAD_DIM)
    positions = row_index * query_len + jnp.arange(query_len, dtype=jnp.int32)
    cos_table, sin_table = rope_tables(positions, HEAD_DIM)
    queries = proj_qkv[:, :, :repeat]
    keys_raw = proj_qkv[:, :, repeat]
    vals_raw = proj_qkv[:, :, repeat + 1]
    queries_rot = (
        (queries * cos_table[:, None, None] + rotate_half(queries) * sin_table[:, None, None])
        * score_scale
    ).astype(jnp.bfloat16)
    keys_rot = (keys_raw * cos_table[:, None] + rotate_half(keys_raw) * sin_table[:, None]).astype(
        jnp.bfloat16
    )
    key_value = jnp.concatenate(
        [
            keys_rot.reshape(query_len, kv_cols),
            vals_raw.astype(jnp.bfloat16).reshape(query_len, kv_cols),
        ],
        axis=1,
    )
    key_value_all = row_rows(key_value)
    keys_all = key_value_all[:, :kv_cols].reshape(seq_len, groups_local, HEAD_DIM)
    values_all = key_value_all[:, kv_cols:].reshape(seq_len, groups_local, HEAD_DIM)
    causal = jnp.arange(seq_len, dtype=jnp.int32)[None, :] <= positions[:, None]
    scores = jnp.einsum("qgrd,kgd->grqk", queries_rot, keys_all, preferred_element_type=jnp.float32)
    exp_scores = jnp.where(causal, jnp.exp(scores), 0.0)
    log_total = jnp.log(jnp.sum(exp_scores, axis=-1, keepdims=True))
    attn_probs = jnp.where(causal, jnp.exp(scores - log_total), 0.0)
    probs_b = attn_probs.astype(jnp.bfloat16)
    attended = (
        jnp.einsum("grqk,kgd->qgrd", probs_b, values_all, preferred_element_type=jnp.float32)
        .astype(jnp.bfloat16)
        .reshape(query_len, -1)
    )
    attended_all = row_rows(attended)

    def attn_term(first_row, row_count):
        return jnp.dot(attended_all, w_out, preferred_element_type=jnp.float32)

    hidden_res = inputs_f + col_terms(attn_term, tok_local)
    gained = hidden_res * ffn_gain
    square_two, router_part = lax.psum(
        (
            jnp.sum(hidden_res * hidden_res, axis=1),
            jnp.dot(gained, w_router, precision=lax.Precision.HIGHEST),
        ),
        "row",
    )
    inv_rms_two = lax.rsqrt(square_two / model_width + epsilon)[:, None]
    unit_two = hidden_res * inv_rms_two
    normed_two_f = gained * inv_rms_two
    normed_two = normed_two_f.astype(jnp.bfloat16)
    logits = router_part * inv_rms_two
    routes_local = lax.dynamic_slice_in_dim(routes, col_index * tok_local, tok_local, 0)
    chosen_mask = (
        routes_local[:, :, None] == jnp.arange(experts, dtype=jnp.int32)[None, None, :]
    ).astype(jnp.float32)
    chosen = jnp.sum(chosen_mask * logits[:, None, :], axis=2)
    exp_chosen = jnp.exp(chosen)
    gate_weights = exp_chosen / jnp.sum(exp_chosen, axis=1, keepdims=True)
    normed_two_all = col_rows(normed_two)
    slot_of_pair, pair_of_slot, filled = slot_tables(routes, experts, capacity)
    token_of_slot = pair_of_slot // top_count
    slot_rows = jnp.where(filled[:, None] > 0, normed_two_all[token_of_slot], 0)
    w_both = jnp.concatenate([w_gate, w_up], axis=2)
    row_block = slot_rows.reshape(
        slots_local * lax.axis_size("row") // capacity, capacity, width_local
    )
    pre_act = lax.psum_scatter(
        jnp.einsum("ecd,edf->ecf", row_block, w_both, preferred_element_type=jnp.float32).reshape(
            slots_local * lax.axis_size("row"), 2 * ffn_local
        ),
        "row",
        scatter_dimension=0,
        tiled=True,
    )
    gate_pre = pre_act[:, :ffn_local]
    up_val = pre_act[:, ffn_local:]
    sigmoid_gate = jax.nn.sigmoid(gate_pre)
    activated = (gate_pre * sigmoid_gate * up_val).astype(jnp.bfloat16)
    activated_all = row_rows(activated)
    down_slots = jnp.einsum(
        "ecf,efd->ecd",
        activated_all.reshape(experts, capacity, ffn_local),
        w_down,
        preferred_element_type=jnp.float32,
    ).reshape(experts * capacity, width_local)
    pair_out = down_slots[slot_of_pair]
    pair_local = col_terms(slicer(pair_out), tok_local * top_count).reshape(
        tok_local, top_count, width_local
    )
    block_output = (hidden_res + jnp.sum(gate_weights[:, :, None] * pair_local, axis=1)).astype(
        jnp.bfloat16
    )
    grad_f = out_grad.astype(jnp.float32)
    gate_grads = row_total(jnp.sum(grad_f[:, None, :] * pair_local, axis=2))
    gate_mix = gate_weights * (
        gate_grads - jnp.sum(gate_weights * gate_grads, axis=1, keepdims=True)
    )
    logit_grads = jnp.sum(gate_mix[:, :, None] * chosen_mask, axis=1)
    pair_grad = (
        (gate_weights[:, :, None] * grad_f[:, None, :])
        .astype(jnp.bfloat16)
        .reshape(tok_local * top_count, width_local)
    )
    pair_grad_all = col_rows(pair_grad)
    slot_grad = jnp.where(filled[:, None] > 0, pair_grad_all[pair_of_slot], 0)

    def act_term(first_row, row_count):
        row_block = slot_grad.reshape(row_count // capacity, capacity, width_local)
        return jnp.einsum(
            "ecd,efd->ecf", row_block, w_down, preferred_element_type=jnp.float32
        ).reshape(row_count, ffn_local)

    act_grad = row_terms(act_term, slots_local)
    gate_pre_grad = act_grad * up_val * sigmoid_gate * (1.0 + gate_pre * (1.0 - sigmoid_gate))
    up_grad = act_grad * gate_pre * sigmoid_gate
    pre_grad = jnp.concatenate([gate_pre_grad, up_grad], axis=1).astype(jnp.bfloat16)
    pre_grad_all = row_rows(pre_grad).reshape(experts, capacity, 2 * ffn_local)
    down_grad = jnp.einsum(
        "ecf,ecd->efd",
        activated_all.reshape(experts, capacity, ffn_local),
        slot_grad.reshape(experts, capacity, width_local),
        preferred_element_type=jnp.float32,
    )
    both_grad = jnp.einsum(
        "ecd,ecf->edf",
        slot_rows.reshape(experts, capacity, width_local),
        pre_grad_all,
        preferred_element_type=jnp.float32,
    )
    slot_back = jnp.einsum(
        "ecf,edf->ecd", pre_grad_all, w_both, preferred_element_type=jnp.float32
    ).reshape(experts * capacity, width_local)
    token_back = jnp.sum(slot_back[slot_of_pair].reshape(seq_len, top_count, width_local), axis=1)
    normed_grad = col_terms(slicer(token_back), tok_local)
    normed_grad = normed_grad + jnp.dot(logit_grads, w_router.T, precision=lax.Precision.HIGHEST)
    ffn_gain_part = jnp.sum(normed_grad * unit_two, axis=0)
    router_part_grad = jnp.dot(normed_two_f.T, logit_grads, precision=lax.Precision.HIGHEST)
    unit_grad_two = normed_grad * ffn_gain
    inner_two = row_total(jnp.sum(unit_grad_two * unit_two, axis=1))
    residual_grad = grad_f + inv_rms_two * (
        unit_grad_two - unit_two * (inner_two / model_width)[:, None]
    )
    residual_b = residual_grad.astype(jnp.bfloat16)
    residual_all = col_rows(residual_b)
    out_proj_grad = jnp.einsum(
        "th,td->hd", attended_all, residual_all, preferred_element_type=jnp.float32
    )

    def attn_back_term(first_row, row_count):
        return jnp.einsum("td,hd->th", residual_all, w_out, preferred_element_type=jnp.float32)

    attended_grad = (
        row_terms(attn_back_term, query_len)
        .astype(jnp.bfloat16)
        .reshape(query_len, groups_local, repeat, HEAD_DIM)
    )
    prob_grad = jnp.einsum(
        "qgrd,kgd->grqk", attended_grad, values_all, preferred_element_type=jnp.float32
    )
    prob_inner = jnp.sum(attn_probs * prob_grad, axis=-1, keepdims=True)
    score_grad = (attn_probs * (prob_grad - prob_inner)).astype(jnp.bfloat16)
    query_grad = jnp.einsum(
        "grqk,kgd->qgrd", score_grad, keys_all, preferred_element_type=jnp.float32
    )
    key_part = jnp.einsum(
        "grqk,qgrd->kgd", score_grad, queries_rot, preferred_element_type=jnp.float32
    )
    value_part = jnp.einsum(
        "grqk,qgrd->kgd", probs_b, attended_grad, preferred_element_type=jnp.float32
    )
    kv_part = jnp.concatenate(
        [key_part.reshape(seq_len, kv_cols), value_part.reshape(seq_len, kv_cols)], axis=1
    )
    kv_grad = row_terms(slicer(kv_part), query_len)
    key_grad = kv_grad[:, :kv_cols].reshape(query_len, groups_local, HEAD_DIM)
    value_grad = kv_grad[:, kv_cols:].reshape(query_len, groups_local, HEAD_DIM)
    query_back = (
        query_grad * cos_table[:, None, None] - rotate_half(query_grad * sin_table[:, None, None])
    ) * score_scale
    key_back = key_grad * cos_table[:, None] - rotate_half(key_grad * sin_table[:, None])
    qkv_grad = (
        jnp.concatenate([query_back, key_back[:, :, None], value_grad[:, :, None]], axis=2)
        .reshape(query_len, -1)
        .astype(jnp.bfloat16)
    )
    qkv_grad_all = row_rows(qkv_grad)
    qkv_weight_part = jnp.einsum(
        "td,tc->dc", normed_all, qkv_grad_all, preferred_element_type=jnp.float32
    )

    def norm_back_term(first_row, row_count):
        return jnp.einsum("tc,dc->td", qkv_grad_all, w_qkv, preferred_element_type=jnp.float32)

    normed_one_grad = col_terms(norm_back_term, tok_local)
    attn_gain_part = jnp.sum(normed_one_grad * unit_one, axis=0)
    unit_grad_one = normed_one_grad * attn_gain
    inner_one = row_total(jnp.sum(unit_grad_one * unit_one, axis=1))
    input_grad = residual_grad + inv_rms_one * (
        unit_grad_one - unit_one * (inner_one / model_width)[:, None]
    )
    grad_qkv, grad_out = (
        lax.psum(qkv_weight_part.astype(jnp.bfloat16), "dp").astype(jnp.float32),
        lax.psum(out_proj_grad.astype(jnp.bfloat16), "dp").astype(jnp.float32),
    )
    grad_attn_gain, grad_ffn_gain, grad_router = lax.psum(
        (attn_gain_part, ffn_gain_part, router_part_grad), ("dp", "col")
    )
    grad_gate, grad_up, grad_down = (
        lax.psum_scatter(
            both_grad[:, :, :ffn_local].astype(jnp.bfloat16), "dp", scatter_dimension=0, tiled=True
        ).astype(jnp.float32),
        lax.psum_scatter(
            both_grad[:, :, ffn_local:].astype(jnp.bfloat16), "dp", scatter_dimension=0, tiled=True
        ).astype(jnp.float32),
        lax.psum_scatter(
            down_grad.astype(jnp.bfloat16), "dp", scatter_dimension=0, tiled=True
        ).astype(jnp.float32),
    )
    return (
        block_output,
        input_grad,
        grad_attn_gain,
        grad_qkv,
        grad_out,
        grad_ffn_gain,
        grad_router,
        grad_gate,
        grad_up,
        grad_down,
    )


def from_blocks(blocks):
    row_blocks, col_blocks, height, width = blocks.shape
    return blocks.transpose(0, 2, 1, 3).reshape(row_blocks * height, col_blocks * width)


def to_blocks(full_array, height, width):
    rows, cols = full_array.shape
    return full_array.reshape(rows // height, height, cols // width, width).transpose(0, 2, 1, 3)


def expert_owner(
    block_input, attn_gain, w_qkv, w_out, ffn_gain, w_router, w_gate, w_up, w_down, routes, out_grad
):
    tok_local, width_local = block_input.shape
    dp_size, row_size, col_size = (lax.axis_size(name) for name in ("dp", "row", "col"))
    model_width = width_local * row_size
    seq_len = routes.shape[0]
    tokens = seq_len * dp_size
    experts = w_gate.shape[0]
    ffn_local = w_gate.shape[2]
    ffn = ffn_local * col_size
    repeat = HEADS // KV_HEADS
    groups_local = KV_HEADS // col_size
    head_cols = groups_local * repeat * HEAD_DIM
    dp_index, row_index, col_index = (lax.axis_index(name) for name in ("dp", "row", "col"))
    score_scale = HEAD_DIM ** (-0.5)
    everyone = ("dp", "col", "row")
    peers = ("row", "col")
    owned = experts // dp_size
    own_expert = dp_index * owned + row_index * col_size + col_index
    token_blocks = dp_size * col_size
    tok_share = tokens // (token_blocks * row_size)
    seq_first = dp_index * seq_len
    block_first = (dp_index * col_size + col_index) * tok_local
    share_first = block_first + row_index * tok_share
    width_first = row_index * width_local

    def rows_of(full_array, first_row, count):
        return lax.dynamic_slice_in_dim(full_array, first_row, count, 0)

    def cols_of(full_array, first_col, count):
        return lax.dynamic_slice_in_dim(full_array, first_col, count, 1)

    def after(first, later):
        return lax.optimization_barrier((first, later))[1]

    def swap(blocks, names):
        return lax.all_to_all(blocks, names, 0, 0, tiled=True)

    def to_all(block_array, names, count):
        return swap(jnp.broadcast_to(block_array, (count,) + block_array.shape), names)

    def to_blocks_all(block_array):
        sent_on = to_all(block_array, ("dp", "col"), token_blocks)
        return sent_on.reshape(tokens, block_array.shape[1])

    def summed(blocks, names):
        return jnp.sum(swap(blocks, names).astype(jnp.float32), axis=0)

    def block_sum(full_array):
        blocks = full_array.reshape(token_blocks, tok_local, model_width)
        return summed(blocks, ("dp", "col")).astype(jnp.bfloat16)

    small = jnp.concatenate([w_router.T, attn_gain[None], ffn_gain[None]], axis=0)
    small_all = to_all(small, "row", row_size).transpose(1, 0, 2).reshape(-1, model_width)
    wide_input = to_all(block_input, "row", row_size).transpose(1, 0, 2)
    inputs_all = to_blocks_all(wide_input.reshape(tok_local, model_width))
    inputs_f = inputs_all.astype(jnp.float32)
    w_qkv_all = lax.all_gather(w_qkv, "row", axis=0, tiled=True)
    w_router_all = small_all[:experts].T
    attn_gain_all = small_all[experts]
    ffn_gain_all = small_all[experts + 1]
    routes_all = lax.all_gather(routes, "dp", axis=0, tiled=True)
    w_out_all = from_blocks(
        lax.all_gather(after(w_qkv_all, w_out), ("col", "row"), axis=0).reshape(
            col_size, row_size, w_out.shape[0], width_local
        )
    )
    grad_f = from_blocks(
        lax.all_gather(after(w_out_all, out_grad), everyone, axis=0).reshape(
            token_blocks, row_size, tok_local, width_local
        )
    ).astype(jnp.float32)

    def own_weight(weight):
        mine = lax.dynamic_slice_in_dim(weight, dp_index * owned, owned, 0)
        moved = lax.all_to_all(mine, peers, 0, 0, tiled=True)
        return moved.reshape((row_size, col_size) + weight.shape[1:])

    gate_own = from_blocks(own_weight(w_gate))
    up_own = from_blocks(own_weight(w_up))
    down_own = from_blocks(own_weight(w_down).transpose(1, 0, 2, 3))

    inv_rms_one = lax.rsqrt(jnp.mean(inputs_f * inputs_f, axis=1, keepdims=True) + epsilon)
    unit_one = inputs_f * inv_rms_one
    normed_one = (unit_one * attn_gain_all).astype(jnp.bfloat16)
    normed_seq = rows_of(normed_one, seq_first, seq_len)
    proj_flat = jnp.dot(normed_seq, w_qkv_all, preferred_element_type=jnp.float32)
    proj_qkv = proj_flat.reshape(seq_len, groups_local, repeat + 2, HEAD_DIM)
    positions = jnp.arange(seq_len, dtype=jnp.int32)
    cos_table, sin_table = rope_tables(positions, HEAD_DIM)
    queries = proj_qkv[:, :, :repeat]
    keys_raw = proj_qkv[:, :, repeat]
    values_all = proj_qkv[:, :, repeat + 1].astype(jnp.bfloat16)
    queries_rot = (
        (queries * cos_table[:, None, None] + rotate_half(queries) * sin_table[:, None, None])
        * score_scale
    ).astype(jnp.bfloat16)
    keys_all = (keys_raw * cos_table[:, None] + rotate_half(keys_raw) * sin_table[:, None]).astype(
        jnp.bfloat16
    )
    causal = positions[None, :] <= positions[:, None]
    scores = jnp.einsum("qgrd,kgd->grqk", queries_rot, keys_all, preferred_element_type=jnp.float32)
    exp_scores = jnp.where(causal, jnp.exp(scores), 0.0)
    log_total = jnp.log(jnp.sum(exp_scores, axis=-1, keepdims=True))
    attn_probs = jnp.where(causal, jnp.exp(scores - log_total), 0.0)
    probs_b = attn_probs.astype(jnp.bfloat16)
    attended = (
        jnp.einsum("grqk,kgd->qgrd", probs_b, values_all, preferred_element_type=jnp.float32)
        .astype(jnp.bfloat16)
        .reshape(seq_len, head_cols)
    )
    attended_all = from_blocks(
        to_all(attended, ("dp", "col"), token_blocks).reshape(
            dp_size, col_size, seq_len, head_cols
        )
    )
    hidden_res = inputs_f + jnp.dot(attended_all, w_out_all, preferred_element_type=jnp.float32)
    inv_rms_two = lax.rsqrt(jnp.mean(hidden_res * hidden_res, axis=1, keepdims=True) + epsilon)
    unit_two = hidden_res * inv_rms_two
    normed_two_f = unit_two * ffn_gain_all
    normed_two = normed_two_f.astype(jnp.bfloat16)
    logits = jnp.dot(normed_two_f, w_router_all, precision=lax.Precision.HIGHEST)
    chosen_mask = jnp.any(
        routes_all[:, :, None] == jnp.arange(experts, dtype=jnp.int32)[None, None, :], axis=1
    )
    exp_chosen = jnp.where(chosen_mask, jnp.exp(logits), 0.0)
    gate_weights = exp_chosen / jnp.sum(exp_chosen, axis=1, keepdims=True)
    gate_own_weight = cols_of(gate_weights, own_expert, 1)

    gate_pre = jnp.dot(normed_two, gate_own, preferred_element_type=jnp.float32)
    up_val = jnp.dot(normed_two, up_own, preferred_element_type=jnp.float32)
    sigmoid_gate = jax.nn.sigmoid(gate_pre)
    activated = (gate_pre * sigmoid_gate * up_val).astype(jnp.bfloat16)
    pair_out = jnp.dot(activated, down_own, preferred_element_type=jnp.float32)
    gate_grads = to_all(
        jnp.sum(grad_f * pair_out, axis=1).reshape(-1, 128), ("dp", "row", "col"), experts
    ).reshape(experts, tokens).T
    gate_mix = gate_weights * (
        gate_grads - jnp.sum(gate_weights * gate_grads, axis=1, keepdims=True)
    )
    pair_grad = (gate_own_weight * grad_f).astype(jnp.bfloat16)
    act_grad = lax.dot_general(
        pair_grad, down_own, (((1,), (1,)), ((), ())), preferred_element_type=jnp.float32
    )
    gate_pre_grad = (
        act_grad * up_val * sigmoid_gate * (1.0 + gate_pre * (1.0 - sigmoid_gate))
    ).astype(jnp.bfloat16)
    up_grad = (act_grad * gate_pre * sigmoid_gate).astype(jnp.bfloat16)
    token_back = lax.dot_general(
        gate_pre_grad, gate_own, (((1,), (1,)), ((), ())), preferred_element_type=jnp.float32
    ) + lax.dot_general(
        up_grad, up_own, (((1,), (1,)), ((), ())), preferred_element_type=jnp.float32
    )
    back_block = block_sum(token_back.astype(jnp.bfloat16))
    back_share = summed(back_block.reshape(row_size, tok_share, model_width), "row")
    normed_grad = back_share + jnp.dot(
        rows_of(gate_mix, share_first, tok_share), w_router_all.T, precision=lax.Precision.HIGHEST
    )
    unit_share = rows_of(unit_two, share_first, tok_share)
    ffn_gain_part = jnp.sum(normed_grad * unit_share, axis=0)
    unit_grad_two = normed_grad * ffn_gain_all
    residual_share = rows_of(grad_f, share_first, tok_share) + rows_of(
        inv_rms_two, share_first, tok_share
    ) * (unit_grad_two - unit_share * jnp.mean(unit_grad_two * unit_share, axis=1, keepdims=True))
    residual_block = to_all(residual_share.astype(jnp.bfloat16), "row", row_size)
    residual_all = to_blocks_all(residual_block.reshape(tok_local, model_width))

    moe_block = block_sum(after(residual_all, (gate_own_weight * pair_out).astype(jnp.bfloat16)))
    moe_own = summed(
        moe_block.reshape(tok_local, row_size, width_local).transpose(1, 0, 2), "row"
    )
    own_hidden = cols_of(rows_of(hidden_res, block_first, tok_local), width_first, width_local)
    block_output = (own_hidden + moe_own).astype(jnp.bfloat16)

    def expert_grad(blocks):
        return swap(blocks, peers).astype(jnp.float32)

    def turned(left, right):
        return lax.dot_general(
            left, right, (((0,), (0,)), ((), ())), preferred_element_type=jnp.float32
        )

    def sent(blocks):
        return blocks.reshape((row_size * col_size,) + blocks.shape[2:])

    grad_down = expert_grad(
        sent(
            to_blocks(
                turned(activated, pair_grad).astype(jnp.bfloat16), ffn_local, width_local
            ).transpose(1, 0, 2, 3)
        )
    )
    grad_gate = expert_grad(
        sent(to_blocks(turned(normed_two, gate_pre_grad).astype(jnp.bfloat16), width_local, ffn_local))
    )
    grad_up = expert_grad(
        sent(to_blocks(turned(normed_two, up_grad).astype(jnp.bfloat16), width_local, ffn_local))
    )
    grad_router = lax.dot_general(
        cols_of(normed_two_f, width_first, width_local),
        gate_mix,
        (((0,), (0,)), ((), ())),
        precision=lax.Precision.HIGHEST,
    )

    grad_out = turned(
        cols_of(attended_all, col_index * head_cols, head_cols),
        cols_of(residual_all, width_first, width_local),
    )
    attended_grad = (
        lax.dot_general(
            rows_of(residual_all, seq_first, seq_len),
            rows_of(w_out_all, col_index * head_cols, head_cols),
            (((1,), (1,)), ((), ())),
            preferred_element_type=jnp.float32,
        )
        .astype(jnp.bfloat16)
        .reshape(seq_len, groups_local, repeat, HEAD_DIM)
    )
    prob_grad = jnp.einsum(
        "qgrd,kgd->grqk", attended_grad, values_all, preferred_element_type=jnp.float32
    )
    prob_inner = jnp.sum(attn_probs * prob_grad, axis=-1, keepdims=True)
    score_grad = (attn_probs * (prob_grad - prob_inner)).astype(jnp.bfloat16)
    query_grad = jnp.einsum(
        "grqk,kgd->qgrd", score_grad, keys_all, preferred_element_type=jnp.float32
    )
    key_grad = jnp.einsum(
        "grqk,qgrd->kgd", score_grad, queries_rot, preferred_element_type=jnp.float32
    )
    value_grad = jnp.einsum(
        "grqk,qgrd->kgd", probs_b, attended_grad, preferred_element_type=jnp.float32
    )
    query_back = (
        query_grad * cos_table[:, None, None] - rotate_half(query_grad * sin_table[:, None, None])
    ) * score_scale
    key_back = key_grad * cos_table[:, None] - rotate_half(key_grad * sin_table[:, None])
    qkv_grad = (
        jnp.concatenate([query_back, key_back[:, :, None], value_grad[:, :, None]], axis=2)
        .reshape(seq_len, -1)
        .astype(jnp.bfloat16)
    )
    qkv_part = turned(cols_of(normed_seq, width_first, width_local), qkv_grad)
    grad_qkv = jnp.sum(
        to_all(qkv_part.astype(jnp.bfloat16), "dp", dp_size).astype(jnp.float32), axis=0
    )
    norm_back = lax.dot_general(
        qkv_grad, w_qkv, (((1,), (1,)), ((), ())), preferred_element_type=jnp.float32
    )
    unit_own = cols_of(rows_of(unit_one, seq_first, seq_len), width_first, width_local)
    attn_gain_part = jnp.sum(norm_back * unit_own, axis=0)
    inner_part = jnp.sum(qkv_grad.astype(jnp.float32) * proj_flat, axis=1, keepdims=True)
    input_part = rows_of(inv_rms_one, seq_first, seq_len) * (
        norm_back * attn_gain - unit_own * (inner_part / model_width)
    )
    own_residual = cols_of(rows_of(residual_all, block_first, tok_local), width_first, width_local)
    input_grad = own_residual.astype(jnp.float32) + summed(
        input_part.astype(jnp.bfloat16).reshape(col_size, tok_local, width_local), "col"
    )
    attn_gain_wide = lax.dynamic_update_slice_in_dim(
        jnp.zeros((model_width,), jnp.float32), attn_gain_part, width_first, 0
    )
    gain_parts = jnp.stack([attn_gain_wide, ffn_gain_part]).reshape(2, row_size, width_local)
    gains_own = summed(
        jnp.broadcast_to(
            gain_parts.transpose(1, 0, 2)[None, :, None],
            (dp_size, row_size, col_size, 2, width_local),
        ).reshape(experts, 2, width_local),
        ("dp", "row", "col"),
    )
    return (
        block_output,
        input_grad,
        gains_own[0],
        grad_qkv,
        grad_out,
        gains_own[1],
        grad_router,
        grad_gate,
        grad_up,
        grad_down,
    )


def solution(mesh):
    in_specs = (
        P(("dp", "col"), "row"),
        P("row"),
        P("row", "col"),
        P("col", "row"),
        P("row"),
        P("row", None),
        P(None, "row", "col"),
        P(None, "row", "col"),
        P(None, "col", "row"),
        P("dp", None),
        P(("dp", "col"), "row"),
    )
    out_specs = (
        P(("dp", "col"), "row"),
        P(("dp", "col"), "row"),
        P("row"),
        P("row", "col"),
        P("col", "row"),
        P("row"),
        P("row", None),
        P("dp", "row", "col"),
        P("dp", "row", "col"),
        P("dp", "col", "row"),
    )
    sizes = dict(mesh.shape)
    one_expert_each = sizes["dp"] * sizes["row"] * sizes["col"] == EXPERTS
    return jax.shard_map(
        expert_owner if one_expert_each else per_device, mesh=mesh, in_specs=in_specs, out_specs=out_specs, check_vma=False
    )
```
